256 devices in a mesh: row: 16 (over y, z_hi), col: 16 (over x, z_lo, core).
Axes of the slice: x: 4, y: 4, z: 8 (z_hi: 4, z_lo: 2; z = z_hi * 2 + z_lo), core: 2. Of those that a mesh axis runs over, the one named last changes fastest.
Arguments:
- fit_tiles: bfloat16 [32, 96, 128, 128], P('row', 'col'), may hold values from -6 to 6
- aux_list: int32 [32, 96], P('row', 'col'), may hold values from 0 to 11, as said below
- aux_count: int32 [32, 16], P('row', 'col'), may hold values from 1 to 6, as said below
- metric: bfloat16 [192, 128, 128], P('col', 'row'), may hold values from -0.5 to 0.5
Outputs:
- exchange: float32 [4096, 4096], P('col', 'row')
The draws below stay inside these ranges and needn't reach their ends.
Inputs may be any that keep to these rules, and one draw needn't show every extreme that they name: `aux_list`: within one atom block and one col shard, the first 6 slots name distinct auxiliary blocks. `aux_count`: counts follow a density per atom block; the largest is reached in every draw.
All inputs are finite; a program needn't handle non-finite values.
Results may differ from the reference program's by a relative error of at most 0.0015.
Values may be sent and summed in bfloat16 or wider, within the bound.
No kernel may reach another device: no remote copies, remote signals or barrier semaphores. Data moves between devices by JAX's collectives and lax.ppermute only.
A program may use at most 64 MiB of HBM per device.

```python
import jax
import jax.numpy as jnp
from jax import lax

BS = 128
AUXB = 128
QB = 12
QS = 6
NS = 32
NQ = 192
NF = 4096
N_COL = 16


def draw_aux_list(key, part):
    scores = jax.random.randint(key, (NS, N_COL, QB), 0, 1 << 20) * QB + jnp.arange(QB, dtype=jnp.int32)
    order = jnp.argsort(scores, axis=-1, stable=True).astype(jnp.int32)
    return order[:, :, :QS].reshape(NS, N_COL * QS)


def draw_aux_count(key, part):
    first = jax.random.fold_in(key, 11)
    second = jax.random.fold_in(key, 12)
    density = jax.random.randint(first, (NS, 1), 1, QS + 1)
    jitter = jax.random.randint(second, (NS, N_COL), 0, 2)
    counts = jnp.clip(density - jitter, 1, QS)
    corner = (jnp.arange(NS)[:, None] == 0) & (jnp.arange(N_COL)[None, :] == 0)
    return jnp.where(corner, QS, counts).astype(jnp.int32)


def block_levels(stream_key, shape, split, low, high):
    def one(position, parts):
        steps = jax.random.uniform(jax.random.fold_in(jax.random.fold_in(stream_key, 6), position), (parts,), jnp.float32, low / len(split), high / len(split))
        return jnp.repeat(jnp.exp(steps), shape[position] // parts).reshape((-1,) + (1,) * (len(shape) - position - 1))

    gain = one(*split[0])
    for cut in split[1:]:
        gain = gain * one(*cut)
    return gain


def noise(stream_key, extent, scale, reach, cuts=(), kind=jnp.bfloat16):
    drawn = jax.random.normal(stream_key, extent, jnp.float32) * scale
    if len(cuts) > 0:
        drawn = block_levels(stream_key, extent, cuts, -0.22, 0.18) * drawn
    return jnp.clip(drawn, min=-reach, max=reach).astype(kind)


def setup_inputs(seed: int = 0) -> dict:
    seeds = jax.random.split(jax.random.key(seed), 5)
    return {
        "fit_tiles": noise(seeds[0], (NS, N_COL * QS, BS, AUXB), 1.0, 6.0, ((0, 16), (1, 16))),
        "aux_list": draw_aux_list(jax.random.fold_in(seeds[4], 71), 0),
        "aux_count": draw_aux_count(jax.random.fold_in(seeds[4], 71), 0),
        "metric": noise(seeds[3], (NQ, AUXB, AUXB), AUXB ** -0.5, 0.5, ((0, 16), (1, 16))),
    }


def reference(fit_tiles, aux_list, aux_count, metric):
    slots = jnp.arange(N_COL * QS, dtype=jnp.int32)
    shard = slots // QS
    local = slots % QS
    live = local[None, :] < aux_count[:, shard]
    qid = (shard[None, :] * QB + aux_list).astype(jnp.int32)

    def one_block(items):
        tiles, ids, alive = items
        mats = metric[ids].astype(jnp.float32)
        fitted = jnp.einsum("smk,skn->smn", tiles.astype(jnp.float32), mats).astype(jnp.bfloat16)
        onehot = ((ids[:, None] == jnp.arange(NQ, dtype=jnp.int32)[None, :]) & alive[:, None]).astype(jnp.float32)
        return jnp.einsum("sq,smn->mqn", onehot, fitted.astype(jnp.float32))

    dense = lax.map(one_block, (fit_tiles, qid, live))
    dense = dense.reshape(NF, NQ * AUXB)
    total = jnp.dot(dense, dense.T, precision=lax.Precision.HIGHEST)
    return total * (1.0 / (QS * N_COL * AUXB) ** 0.5)
```

```python
import functools

import jax
import jax.numpy as jnp
from jax import lax
from jax.experimental import pallas as pl
from jax.experimental.pallas import tpu as pltpu
from jax.sharding import Mesh, PartitionSpec as P


AUXB = 128
BS = 128
QS = 6
QB = 12
NA = 2
ROWS = NA * BS
WIDE = (QB + 1) * AUXB
USED = QB * AUXB
MROWS = 8
HALF = QS * BS
LISTS = 16
SECOND = HALF + LISTS
PAY = SECOND + HALF
F32 = jnp.float32
BF16 = jnp.bfloat16

SMEM = pl.BlockSpec(memory_space=pltpu.SMEM)
VMEM = pl.BlockSpec(memory_space=pltpu.VMEM)
PARAMS = pltpu.CompilerParams(vmem_limit_bytes=14 << 20)


def ring(n, k):
    return [(i, (i + k) % n) for i in range(n)]


def back(i, k):
    return lax.rem(i - k + 4, 4)


def pack_kernel(lists, counts, tiles, out):
    out[0:HALF, :] = tiles[0:HALF, :]
    out[SECOND:PAY, :] = tiles[HALF : 2 * HALF, :]
    lane = lax.broadcasted_iota(jnp.int32, (LISTS, AUXB), 1)
    row = jnp.full((LISTS, AUXB), QB, jnp.int32)
    for a in range(NA):
        for s in range(QS):
            q = jnp.where(s < counts[a, 0], lists[a, s], QB)
            row = jnp.where(lane == a * QS + s, q, row)
    out[HALF:SECOND, :] = row.astype(F32).astype(BF16)


def pack(aux_list, aux_count, tiles):
    return pl.pallas_call(
        pack_kernel,
        out_shape=jax.ShapeDtypeStruct((PAY, AUXB), BF16),
        in_specs=[SMEM, SMEM, VMEM],
        out_specs=VMEM,
        compiler_params=PARAMS,
        name="pack",
    )(aux_list, aux_count, tiles)


def line_kernel(sc_ref, m0, m1, m2, m3, out):
    zh = sc_ref[1]
    for src in range(4):
        k = back(zh, src)
        near = jnp.where(k == 0, m0[...].astype(F32), m1[...].astype(F32))
        far = jnp.where(k == 2, m2[...].astype(F32), m3[...].astype(F32))
        part = jnp.where(k < 2, near, far)
        out[:, src * MROWS : (src + 1) * MROWS, :] = part.astype(BF16)


def line(sc, parts):
    return pl.pallas_call(
        line_kernel,
        out_shape=jax.ShapeDtypeStruct((QB, 4 * MROWS, AUXB), BF16),
        in_specs=[SMEM] + [VMEM] * 4,
        out_specs=VMEM,
        compiler_params=PARAMS,
        name="line",
    )(sc, *parts)


def fill(tiles, start, met, lists, row, first, dense, base):
    for i in range(QS):
        q = lists[row, first + i]
        at = start + i * BS
        fitted = jnp.dot(tiles[at : at + BS, :], met[q], preferred_element_type=F32)
        cols = pl.ds(pl.multiple_of(q * AUXB, AUXB), AUXB)
        dense[pl.ds(pl.multiple_of(base, BS), BS), cols] = fitted.astype(BF16)


def fill_block(tiles, met, lists, row, dense, base):
    fill(tiles, 0, met, lists, row, 0, dense, base)
    fill(tiles, SECOND, met, lists, row, QS, dense, base + BS)


def list_row(tiles, at):
    return tiles[at : at + LISTS, :].astype(F32)[0:1, :].astype(jnp.int32)


def build_kernel(sc_ref, t0, t1, t2, t3, z1, z3, s0, s1, s2, s3, dy, dz, met, lv, ls, sem):
    y, zh = sc_ref[0], sc_ref[1]
    for n, t in enumerate((t0, t1, t2, t3, z1, z3)):
        lv[n : n + 1, :] = list_row(t, HALF)
    copy = pltpu.make_async_copy(lv, ls, sem)
    copy.start()
    for k, s in enumerate((s0, s1, s2, s3)):
        at = pl.multiple_of(back(y, k) * 4 * MROWS, 4 * MROWS)
        met[0:QB, pl.ds(at, 4 * MROWS), :] = s[...]
    dy[...] = jnp.zeros_like(dy)
    dz[...] = jnp.zeros_like(dz)
    copy.wait()
    fill_block(t0, met, ls, 0, dy, y * ROWS)
    mine = dy[pl.ds(pl.multiple_of(y * ROWS, ROWS), ROWS), :]
    dz[pl.ds(pl.multiple_of(zh * ROWS, ROWS), ROWS), :] = mine
    for k, t in ((1, t1), (2, t2), (3, t3)):
        fill_block(t, met, ls, k, dy, back(y, k) * ROWS)
    for n, k, t in ((4, 1, z1), (5, 3, z3)):
        fill_block(t, met, ls, n, dz, back(zh, k) * ROWS)


def build(sc, tiles, zs, smalls):
    dense = jax.ShapeDtypeStruct((4 * ROWS, WIDE), BF16)
    return pl.pallas_call(
        build_kernel,
        out_shape=(dense, dense, jax.ShapeDtypeStruct((QB + 1, AUXB, AUXB), BF16)),
        in_specs=[SMEM] + [VMEM] * 10,
        out_specs=(VMEM,) * 3,
        scratch_shapes=[
            pltpu.VMEM((8, 128), jnp.int32),
            pltpu.SMEM((8, 128), jnp.int32),
            pltpu.SemaphoreType.DMA,
        ],
        compiler_params=PARAMS,
        name="build",
    )(sc, *tiles, *zs, *smalls)


def gram_kernel(flip, h, sc_ref, dy, dz, met, f1, f3, out, far, lv, ls, sem):
    zh, co = sc_ref[1], sc_ref[2]
    p = 2 * h + (1 - co if flip else co)
    opposite = back(zh, 2)
    factor = 1.0 / (QS * 16 * AUXB) ** 0.5

    def product(rhs):
        for q in range(4):
            lhs = dy[q * ROWS : (q + 1) * ROWS, 0:USED]
            prod = lax.dot_general(
                lhs, rhs, (((1,), (1,)), ((), ())), preferred_element_type=F32
            )
            out[q] = prod * factor

    @pl.when(p == opposite)
    def _():
        lv[0:1, :] = list_row(f1, HALF)
        copy = pltpu.make_async_copy(lv, ls, sem)
        copy.start()
        far[...] = jnp.zeros_like(far)
        copy.wait()
        fill(f1, 0, met, ls, 0, 0, far, 0)
        fill(f3, LISTS, met, ls, 0, QS, far, BS)
        product(far[:, 0:USED])

    @pl.when(p != opposite)
    def _():
        product(dz[pl.ds(pl.multiple_of(p * ROWS, ROWS), ROWS), 0:USED])


def gram(flip, h, sc, dy, dz, met, f1, f3):
    return pl.pallas_call(
        functools.partial(gram_kernel, flip, h),
        out_shape=jax.ShapeDtypeStruct((4, ROWS, ROWS), F32),
        in_specs=[SMEM] + [VMEM] * 5,
        out_specs=VMEM,
        scratch_shapes=[
            pltpu.VMEM((ROWS, WIDE), BF16),
            pltpu.VMEM((8, 128), jnp.int32),
            pltpu.SMEM((8, 128), jnp.int32),
            pltpu.SemaphoreType.DMA,
        ],
        compiler_params=PARAMS,
    )(sc, dy, dz, met, f1, f3)


def share_kernel(sc_ref, keep, got, own, out1, out2, out3):
    x = sc_ref[3]
    for k, out in ((0, own), (1, out1), (2, out2), (3, out3)):
        i = lax.rem(x + k, 4)
        out[...] = (keep[i] + got[i]).astype(out.dtype)


def share(sc, keep, got):
    piece = (ROWS, ROWS)
    return pl.pallas_call(
        share_kernel,
        out_shape=(jax.ShapeDtypeStruct(piece, F32),) + (jax.ShapeDtypeStruct(piece, BF16),) * 3,
        in_specs=[SMEM, VMEM, VMEM],
        out_specs=(VMEM,) * 4,
        compiler_params=PARAMS,
        name="share",
    )(sc, keep, got)


def fold_kernel(sc_ref, a0, a1, a2, a3, b0, b1, b2, b3, mine, other):
    low = sc_ref[4] == 0
    first = a0[...] + a1[...].astype(F32) + a2[...].astype(F32) + a3[...].astype(F32)
    second = b0[...] + b1[...].astype(F32) + b2[...].astype(F32) + b3[...].astype(F32)
    mine[...] = jnp.where(low, first, second)
    other[...] = jnp.where(low, second, first).astype(BF16)


def fold(sc, first, second):
    piece = (ROWS, ROWS)
    return pl.pallas_call(
        fold_kernel,
        out_shape=(jax.ShapeDtypeStruct(piece, F32), jax.ShapeDtypeStruct(piece, BF16)),
        in_specs=[SMEM] + [VMEM] * 8,
        out_specs=(VMEM,) * 2,
        compiler_params=PARAMS,
        name="fold",
    )(sc, *first, *second)


def shift(v, axis, perm):
    return lax.ppermute(v, axis, perm)


def local(fit_tiles, aux_list, aux_count, metric):
    sc = jnp.stack([lax.axis_index(n) for n in ("y", "zh", "co", "x", "zl")]).astype(jnp.int32)
    mz = [metric] + [shift(metric, "zh", ring(4, k)) for k in (1, 2, 3)]
    pay = pack(aux_list, aux_count, fit_tiles.reshape(2 * HALF, AUXB))
    z1 = shift(pay, "zh", ring(4, 1))
    z3 = shift(pay, "zh", ring(4, 3))
    ys = [pay] + [shift(pay, "y", ring(4, k)) for k in (1, 2, 3)]
    small = line(sc, mz)
    smalls = [small] + [shift(small, "y", ring(4, k)) for k in (1, 2, 3)]
    f1 = shift(z1[:SECOND], "zh", ring(4, 1))
    f3 = shift(z3[HALF:], "zh", ring(4, 3))

    dy, dz, met = build(sc, ys, [z1, z3], smalls)
    sums = []
    for h in range(2):
        send = gram(True, h, sc, dy, dz, met, f1, f3)
        got = shift(send, "co", ring(2, 1))
        keep = gram(False, h, sc, dy, dz, met, f1, f3)
        own, *shares = share(sc, keep, got)
        sums.append([own] + [shift(shares[k - 1], "x", ring(4, k)) for k in (1, 2, 3)])
    mine, other = fold(sc, *sums)
    total = mine + shift(other, "zl", ring(2, 1)).astype(F32)
    swap = [(a * 4 + b, b * 4 + a) for a in range(4) for b in range(4)]
    return shift(total, ("zh", "zl", "co"), swap)


def solution(mesh):
    fine = Mesh(mesh.devices.reshape(4, 4, 4, 2, 2), ("y", "zh", "x", "zl", "co"))
    row, col = ("y", "zh"), ("x", "zl", "co")
    placed = (P(row, col, None, None), P(row, col), P(row, col), P(col, row, None))

    return jax.shard_map(local, mesh=fine, in_specs=placed, out_specs=P(col, row), check_vma=False)
```

```python
import functools

import jax
import jax.numpy as jnp
from jax import lax
from jax.experimental import pallas as pl
from jax.experimental.pallas import tpu as pltpu
from jax.sharding import Mesh, PartitionSpec as P


AUXB = 128
BS = 128
QS = 6
QB = 12
NA = 2
ROWS = NA * BS
WIDE = (QB + 1) * AUXB
USED = QB * AUXB
MROWS = 8
HALF = QS * BS
PART = QB * MROWS
LIST0 = 4 * PART
SMALL = LIST0 + 16
F32 = jnp.float32
BF16 = jnp.bfloat16

SMEM = pl.BlockSpec(memory_space=pltpu.SMEM)
VMEM = pl.BlockSpec(memory_space=pltpu.VMEM)
PARAMS = pltpu.CompilerParams(vmem_limit_bytes=14 << 20)


def ring(n, k):
    return [(i, (i + k) % n) for i in range(n)]


def back(i, k):
    return lax.rem(i - k + 4, 4)


def pack_kernel(lists, counts, metric, out):
    out[0:PART, :] = metric[...]
    slot = lax.broadcasted_iota(jnp.int32, (NA, QS), 1)
    marked = jnp.where(slot < counts[...], lists[...], QB)
    tail = jnp.concatenate([marked, jnp.zeros((NA, AUXB - QS), jnp.int32)], axis=1)
    tail = jnp.concatenate([tail, jnp.zeros((8 - NA, AUXB), jnp.int32)], axis=0)
    out[PART : PART + 8, :] = tail.astype(F32).astype(BF16)


def pack(aux_list, aux_count, metric):
    return pl.pallas_call(
        pack_kernel,
        out_shape=jax.ShapeDtypeStruct((PART + 8, AUXB), BF16),
        in_specs=[VMEM] * 3,
        out_specs=VMEM,
        compiler_params=PARAMS,
        name="pack",
    )(aux_list, aux_count, metric)


def line_kernel(sc_ref, m0, m1, m2, m3, out):
    zh = sc_ref[1]
    parts = [m[...].astype(F32) for m in (m0, m1, m2, m3)]
    rows = lax.broadcasted_iota(jnp.int32, (8, AUXB), 0)
    tail = jnp.zeros((8, AUXB), F32)
    for src in range(4):
        k = back(zh, src)
        near = jnp.where(k == 0, parts[0], parts[1])
        far = jnp.where(k == 2, parts[2], parts[3])
        part = jnp.where(k < 2, near, far)
        for q in range(QB):
            at = (4 * q + src) * MROWS
            out[at : at + MROWS, :] = part[q * MROWS : (q + 1) * MROWS, :].astype(BF16)
        for a in range(NA):
            tail = jnp.where(rows == NA * src + a, part[PART + a : PART + a + 1, :], tail)
    both = jnp.concatenate([tail, parts[0][PART : PART + 8, :]], axis=0)
    out[LIST0:SMALL, :] = both.astype(BF16)


def line(sc, parts):
    return pl.pallas_call(
        line_kernel,
        out_shape=jax.ShapeDtypeStruct((SMALL, AUXB), BF16),
        in_specs=[SMEM] + [VMEM] * 4,
        out_specs=VMEM,
        compiler_params=PARAMS,
        name="line",
    )(sc, *parts)


def fill(tiles, start, met, lists, row, dense, base):
    for i in range(QS):
        q = lists[row, i]
        at = start + i * BS
        fitted = jnp.dot(tiles[at : at + BS, :], met[q], preferred_element_type=F32)
        cols = pl.ds(pl.multiple_of(q * AUXB, AUXB), AUXB)
        dense[pl.ds(pl.multiple_of(base, BS), BS), cols] = fitted.astype(BF16)


def fill_block(tiles, met, lists, row, dense, base):
    for a in range(NA):
        fill(tiles, a * HALF, met, lists, row + a, dense, base + a * BS)


def read_lists(small):
    return small[LIST0:SMALL, :].astype(F32).astype(jnp.int32)


def build_kernel(sc_ref, t0, t1, t2, t3, z1, z3, s0, s1, s2, s3, dy, dz, met, lv, ls, sem):
    y, zh = sc_ref[0], sc_ref[1]
    for k, s in enumerate((s0, s1, s2, s3)):
        lv[16 * k : 16 * k + 16, :] = read_lists(s)
    copy = pltpu.make_async_copy(lv, ls, sem)
    copy.start()
    for k, s in enumerate((s0, s1, s2, s3)):
        at = pl.multiple_of(back(y, k) * 4 * MROWS, 4 * MROWS)
        met[0:QB, pl.ds(at, 4 * MROWS), :] = s[0:LIST0, :].reshape(QB, 4 * MROWS, AUXB)
    dy[...] = jnp.zeros_like(dy)
    dz[...] = jnp.zeros_like(dz)
    copy.wait()
    fill_block(t0, met, ls, 8, dy, y * ROWS)
    mine = dy[pl.ds(pl.multiple_of(y * ROWS, ROWS), ROWS), :]
    dz[pl.ds(pl.multiple_of(zh * ROWS, ROWS), ROWS), :] = mine
    for k, t in ((1, t1), (2, t2), (3, t3)):
        fill_block(t, met, ls, 16 * k + 8, dy, back(y, k) * ROWS)
    for k, t in ((1, z1), (3, z3)):
        src = back(zh, k)
        fill_block(t, met, ls, NA * src, dz, src * ROWS)


def build(sc, tiles, zs, smalls):
    dense = jax.ShapeDtypeStruct((4 * ROWS, WIDE), BF16)
    return pl.pallas_call(
        build_kernel,
        out_shape=(dense, dense, jax.ShapeDtypeStruct((QB + 1, AUXB, AUXB), BF16)),
        in_specs=[SMEM] + [VMEM] * 10,
        out_specs=(VMEM,) * 3,
        scratch_shapes=[
            pltpu.VMEM((64, 128), jnp.int32),
            pltpu.SMEM((64, 128), jnp.int32),
            pltpu.SemaphoreType.DMA,
        ],
        compiler_params=PARAMS,
        name="build",
    )(sc, *tiles, *zs, *smalls)


def gram_kernel(flip, sc_ref, dy, dz, met, f1, f3, s0, out, far, lv, ls, sem):
    zh, co = sc_ref[1], sc_ref[2]
    parity = 1 - co if flip else co
    opposite = back(zh, 2)
    factor = 1.0 / (QS * 16 * AUXB) ** 0.5

    @pl.when(lax.rem(zh, 2) == parity)
    def _():
        lv[...] = read_lists(s0)
        copy = pltpu.make_async_copy(lv, ls, sem)
        copy.start()
        far[...] = jnp.zeros_like(far)
        copy.wait()
        fill(f1, 0, met, ls, NA * opposite, far, 0)
        fill(f3, 0, met, ls, NA * opposite + 1, far, BS)

    for h in range(2):
        p = 2 * h + parity

        def product(rhs):
            for q in range(4):
                lhs = dy[q * ROWS : (q + 1) * ROWS, 0:USED]
                prod = lax.dot_general(
                    lhs, rhs, (((1,), (1,)), ((), ())), preferred_element_type=F32
                )
                out[q, h] = prod * factor

        @pl.when(p == opposite)
        def _():
            product(far[:, 0:USED])

        @pl.when(p != opposite)
        def _():
            product(dz[pl.ds(pl.multiple_of(p * ROWS, ROWS), ROWS), 0:USED])


def gram(flip, sc, dy, dz, met, f1, f3, small):
    return pl.pallas_call(
        functools.partial(gram_kernel, flip),
        out_shape=jax.ShapeDtypeStruct((4, 2, ROWS, ROWS), F32),
        in_specs=[SMEM] + [VMEM] * 6,
        out_specs=VMEM,
        scratch_shapes=[
            pltpu.VMEM((ROWS, WIDE), BF16),
            pltpu.VMEM((16, 128), jnp.int32),
            pltpu.SMEM((16, 128), jnp.int32),
            pltpu.SemaphoreType.DMA,
        ],
        compiler_params=PARAMS,
        name="send" if flip else "keep",
    )(sc, dy, dz, met, f1, f3, small)


STEPS = tuple((k, w) for w in range(2) for k in range(4))


def share_kernel(sc_ref, keep, got, own, *outs):
    x, zl = sc_ref[3], sc_ref[4]
    for (k, w), out in zip(STEPS, (own,) + outs):
        q, h = lax.rem(x + k, 4), lax.rem(zl + w, 2)
        out[...] = (keep[q, h] + got[q, h]).astype(out.dtype)


def share(sc, keep, got):
    piece = (ROWS, ROWS)
    return pl.pallas_call(
        share_kernel,
        out_shape=(jax.ShapeDtypeStruct(piece, F32),) + (jax.ShapeDtypeStruct(piece, BF16),) * 7,
        in_specs=[SMEM, VMEM, VMEM],
        out_specs=(VMEM,) * 8,
        compiler_params=PARAMS,
        name="share",
    )(sc, keep, got)


def hop(k, w):
    return [(2 * a + b, 2 * ((a + k) % 4) + (b + w) % 2) for a in range(4) for b in range(2)]


def local(fit_tiles, aux_list, aux_count, metric):
    sc = jnp.stack([lax.axis_index(n) for n in ("y", "zh", "co", "x", "zl")]).astype(jnp.int32)
    part = pack(aux_list, aux_count, metric.reshape(PART, AUXB))
    parts = [part] + [lax.ppermute(part, "zh", ring(4, k)) for k in (1, 2, 3)]
    tiles = fit_tiles.reshape(2 * HALF, AUXB)
    z1 = lax.ppermute(tiles, "zh", ring(4, 1))
    z3 = lax.ppermute(tiles, "zh", ring(4, 3))
    ys = [tiles] + [lax.ppermute(tiles, "y", ring(4, k)) for k in (1, 2, 3)]
    small = line(sc, parts)
    smalls = [small] + [lax.ppermute(small, "y", ring(4, k)) for k in (1, 2, 3)]
    f1 = lax.ppermute(z1[:HALF], "zh", ring(4, 1))
    f3 = lax.ppermute(z3[HALF:], "zh", ring(4, 3))

    dy, dz, met = build(sc, ys, [z1, z3], smalls)
    send = gram(True, sc, dy, dz, met, f1, f3, small)
    got = lax.ppermute(send, "co", ring(2, 1))
    keep = gram(False, sc, dy, dz, met, f1, f3, small)
    total, *shares = share(sc, keep, got)
    for (k, w), piece in zip(STEPS[1:], shares):
        total = total + lax.ppermute(piece, ("x", "zl"), hop(k, w)).astype(F32)
    swap = [(a * 4 + b, b * 4 + a) for a in range(4) for b in range(4)]
    return lax.ppermute(total, ("zh", "zl", "co"), swap)


def solution(mesh):
    fine = Mesh(mesh.devices.reshape(4, 4, 4, 2, 2), ("y", "zh", "x", "zl", "co"))
    row, col = ("y", "zh"), ("x", "zl", "co")
    placed = (P(row, col, None, None), P(row, col), P(row, col), P(col, row, None))

    return jax.shard_map(local, mesh=fine, in_specs=placed, out_specs=P(col, row), check_vma=False)
```

```python
import functools

import jax
import jax.numpy as jnp
from jax import lax
from jax.experimental import pallas as pl
from jax.experimental.pallas import tpu as pltpu
from jax.sharding import Mesh, PartitionSpec as P


AUXB = 128
BS = 128
QS = 6
QB = 12
NA = 2
ROWS = NA * BS
WIDE = (QB + 1) * AUXB
USED = QB * AUXB
MROWS = 8
HALF = QS * BS
PART = QB * MROWS
LIST0 = 4 * PART
SMALL = LIST0 + 16
F32 = jnp.float32
BF16 = jnp.bfloat16

SMEM = pl.BlockSpec(memory_space=pltpu.SMEM)
VMEM = pl.BlockSpec(memory_space=pltpu.VMEM)
PARAMS = pltpu.CompilerParams(vmem_limit_bytes=14 << 20)


def ring(n, k):
    return [(i, (i + k) % n) for i in range(n)]


def back(i, k):
    return lax.rem(i - k + 4, 4)


def pack_kernel(lists, counts, metric, out):
    out[0:PART, :] = metric[...]
    slot = lax.broadcasted_iota(jnp.int32, (NA, QS), 1)
    marked = jnp.where(slot < counts[...], lists[...], QB)
    tail = jnp.concatenate([marked, jnp.zeros((NA, AUXB - QS), jnp.int32)], axis=1)
    tail = jnp.concatenate([tail, jnp.zeros((8 - NA, AUXB), jnp.int32)], axis=0)
    out[PART : PART + 8, :] = tail.astype(F32).astype(BF16)


def pack(aux_list, aux_count, metric):
    return pl.pallas_call(
        pack_kernel,
        out_shape=jax.ShapeDtypeStruct((PART + 8, AUXB), BF16),
        in_specs=[VMEM] * 3,
        out_specs=VMEM,
        compiler_params=PARAMS,
        name="pack",
    )(aux_list, aux_count, metric)


def line_kernel(sc_ref, m0, m1, m2, m3, out):
    y = sc_ref[0]
    for k, m in enumerate((m0, m1, m2, m3)):
        at = pl.multiple_of(back(y, k) * PART, 32)
        out[pl.ds(at, PART), :] = m[0:PART, :]
    tail = jnp.concatenate([m0[PART : PART + 8, :].astype(F32), jnp.zeros((8, AUXB), F32)], axis=0)
    out[LIST0:SMALL, :] = tail.astype(BF16)


def line(sc, parts):
    return pl.pallas_call(
        line_kernel,
        out_shape=jax.ShapeDtypeStruct((SMALL, AUXB), BF16),
        in_specs=[SMEM] + [VMEM] * 4,
        out_specs=VMEM,
        compiler_params=PARAMS,
        name="line",
    )(sc, *parts)


def fill(tiles, start, met, lists, row, dense, base):
    for i in range(QS):
        q = lists[row, i]
        at = start + i * BS
        fitted = jnp.dot(tiles[at : at + BS, :], met[q], preferred_element_type=F32)
        cols = pl.ds(pl.multiple_of(q * AUXB, AUXB), AUXB)
        dense[pl.ds(pl.multiple_of(base, BS), BS), cols] = fitted.astype(BF16)


def fill_block(tiles, met, lists, row, dense, base):
    for a in range(NA):
        fill(tiles, a * HALF, met, lists, row + a, dense, base + a * BS)


def read_lists(ref, at):
    return ref[at : at + 8, :].astype(F32).astype(jnp.int32)


def build_kernel(
    sc_ref, t0, t1, t2, t3, z1, z3, p0, p1, p2, p3, s0, s1, s2, s3, dy, dz, met, lv, ls, sem
):
    y, zh = sc_ref[0], sc_ref[1]
    for k, p in enumerate((p0, p1, p2, p3)):
        lv[8 * k : 8 * k + 8, :] = read_lists(p, PART)
    for n, s in ((4, s1), (5, s3)):
        lv[8 * n : 8 * n + 8, :] = read_lists(s, LIST0)
    copy = pltpu.make_async_copy(lv, ls, sem)
    copy.start()
    lines = [s[0:LIST0, :].astype(F32) for s in (s0, s1, s2, s3)]
    for src in range(4):
        k = back(zh, src)
        near = jnp.where(k == 0, lines[0], lines[1])
        far = jnp.where(k == 2, lines[2], lines[3])
        rows = jnp.where(k < 2, near, far)
        for ysrc in range(4):
            for q in range(QB):
                at = ysrc * PART + q * MROWS
                to = (4 * ysrc + src) * MROWS
                met[q, to : to + MROWS, :] = rows[at : at + MROWS, :].astype(BF16)
    dy[...] = jnp.zeros_like(dy)
    dz[...] = jnp.zeros_like(dz)
    copy.wait()
    fill_block(t0, met, ls, 0, dy, y * ROWS)
    mine = dy[pl.ds(pl.multiple_of(y * ROWS, ROWS), ROWS), :]
    dz[pl.ds(pl.multiple_of(zh * ROWS, ROWS), ROWS), :] = mine
    for k, t in ((1, t1), (2, t2), (3, t3)):
        fill_block(t, met, ls, 8 * k, dy, back(y, k) * ROWS)
    for n, k, t in ((4, 1, z1), (5, 3, z3)):
        fill_block(t, met, ls, 8 * n, dz, back(zh, k) * ROWS)


def build(sc, tiles, zs, parts, smalls):
    dense = jax.ShapeDtypeStruct((4 * ROWS, WIDE), BF16)
    return pl.pallas_call(
        build_kernel,
        out_shape=(dense, dense, jax.ShapeDtypeStruct((QB + 1, AUXB, AUXB), BF16)),
        in_specs=[SMEM] + [VMEM] * 14,
        out_specs=(VMEM,) * 3,
        scratch_shapes=[
            pltpu.VMEM((48, 128), jnp.int32),
            pltpu.SMEM((48, 128), jnp.int32),
            pltpu.SemaphoreType.DMA,
        ],
        compiler_params=PARAMS,
        name="build",
    )(sc, *tiles, *zs, *parts, *smalls)


def gram_kernel(flip, sc_ref, dy, dz, met, f1, f3, s2, out, far, lv, ls, sem):
    zh, co = sc_ref[1], sc_ref[2]
    parity = 1 - co if flip else co
    opposite = back(zh, 2)
    factor = 1.0 / (QS * 16 * AUXB) ** 0.5

    @pl.when(lax.rem(zh, 2) == parity)
    def _():
        lv[...] = read_lists(s2, LIST0)
        copy = pltpu.make_async_copy(lv, ls, sem)
        copy.start()
        far[...] = jnp.zeros_like(far)
        copy.wait()
        fill(f1, 0, met, ls, 0, far, 0)
        fill(f3, 0, met, ls, 1, far, BS)

    for h in range(2):
        p = 2 * h + parity

        def product(rhs):
            for q in range(4):
                lhs = dy[q * ROWS : (q + 1) * ROWS, 0:USED]
                prod = lax.dot_general(
                    lhs, rhs, (((1,), (1,)), ((), ())), preferred_element_type=F32
                )
                out[q, h] = prod * factor

        @pl.when(p == opposite)
        def _():
            product(far[:, 0:USED])

        @pl.when(p != opposite)
        def _():
            product(dz[pl.ds(pl.multiple_of(p * ROWS, ROWS), ROWS), 0:USED])


def gram(flip, sc, dy, dz, met, f1, f3, small):
    return pl.pallas_call(
        functools.partial(gram_kernel, flip),
        out_shape=jax.ShapeDtypeStruct((4, 2, ROWS, ROWS), F32),
        in_specs=[SMEM] + [VMEM] * 6,
        out_specs=VMEM,
        scratch_shapes=[
            pltpu.VMEM((ROWS, WIDE), BF16),
            pltpu.VMEM((8, 128), jnp.int32),
            pltpu.SMEM((8, 128), jnp.int32),
            pltpu.SemaphoreType.DMA,
        ],
        compiler_params=PARAMS,
        name="send" if flip else "keep",
    )(sc, dy, dz, met, f1, f3, small)


STEPS = tuple((k, w) for w in range(2) for k in range(4))


def share_kernel(sc_ref, keep, got, own, *outs):
    x, zl = sc_ref[3], sc_ref[4]
    for (k, w), out in zip(STEPS, (own,) + outs):
        q, h = lax.rem(x + k, 4), lax.rem(zl + w, 2)
        out[...] = (keep[q, h] + got[q, h]).astype(out.dtype)


def share(sc, keep, got):
    piece = (ROWS, ROWS)
    return pl.pallas_call(
        share_kernel,
        out_shape=(jax.ShapeDtypeStruct(piece, F32),) + (jax.ShapeDtypeStruct(piece, BF16),) * 7,
        in_specs=[SMEM, VMEM, VMEM],
        out_specs=(VMEM,) * 8,
        compiler_params=PARAMS,
        name="share",
    )(sc, keep, got)


def hop(k, w):
    return [(2 * a + b, 2 * ((a + k) % 4) + (b + w) % 2) for a in range(4) for b in range(2)]


def local(fit_tiles, aux_list, aux_count, metric):
    sc = jnp.stack([lax.axis_index(n) for n in ("y", "zh", "co", "x", "zl")]).astype(jnp.int32)
    part = pack(aux_list, aux_count, metric.reshape(PART, AUXB))
    parts = [part] + [lax.ppermute(part, "y", ring(4, k)) for k in (1, 2, 3)]
    tiles = fit_tiles.reshape(2 * HALF, AUXB)
    z1 = lax.ppermute(tiles, "zh", ring(4, 1))
    z3 = lax.ppermute(tiles, "zh", ring(4, 3))
    ys = [tiles] + [lax.ppermute(tiles, "y", ring(4, k)) for k in (1, 2, 3)]
    small = line(sc, parts)
    smalls = [small] + [lax.ppermute(small, "zh", ring(4, k)) for k in (1, 2, 3)]
    f1 = lax.ppermute(z1[:HALF], "zh", ring(4, 1))
    f3 = lax.ppermute(z3[HALF:], "zh", ring(4, 3))

    dy, dz, met = build(sc, ys, [z1, z3], parts, smalls)
    send = gram(True, sc, dy, dz, met, f1, f3, smalls[2])
    got = lax.ppermute(send, "co", ring(2, 1))
    keep = gram(False, sc, dy, dz, met, f1, f3, smalls[2])
    total, *shares = share(sc, keep, got)
    for (k, w), piece in zip(STEPS[1:], shares):
        total = total + lax.ppermute(piece, ("x", "zl"), hop(k, w)).astype(F32)
    swap = [(a * 4 + b, b * 4 + a) for a in range(4) for b in range(4)]
    return lax.ppermute(total, ("zh", "zl", "co"), swap)


def solution(mesh):
    fine = Mesh(mesh.devices.reshape(4, 4, 4, 2, 2), ("y", "zh", "x", "zl", "co"))
    row, col = ("y", "zh"), ("x", "zl", "co")
    placed = (P(row, col, None, None), P(row, col), P(row, col), P(col, row, None))

    return jax.shard_map(local, mesh=fine, in_specs=placed, out_specs=P(col, row), check_vma=False)
```

```python
import functools

import jax
import jax.numpy as jnp
from jax import lax
from jax.experimental import pallas as pl
from jax.experimental.pallas import tpu as pltpu
from jax.sharding import Mesh, PartitionSpec as P


AUXB = 128
BS = 128
QS = 6
QB = 12
NA = 2
ROWS = NA * BS
WIDE = (QB + 1) * AUXB
USED = QB * AUXB
MROWS = 8
HALF = QS * BS
PART = QB * MROWS
LIST0 = 4 * PART
SMALL = LIST0 + 16
F32 = jnp.float32
BF16 = jnp.bfloat16

SMEM = pl.BlockSpec(memory_space=pltpu.SMEM)
VMEM = pl.BlockSpec(memory_space=pltpu.VMEM)
PARAMS = pltpu.CompilerParams(vmem_limit_bytes=14 << 20)


def ring(n, k):
    return [(i, (i + k) % n) for i in range(n)]


def back(i, k):
    return lax.rem(i - k + 4, 4)


def pack_kernel(lists, counts, metric, out):
    out[0:PART, :] = metric[...]
    slot = lax.broadcasted_iota(jnp.int32, (NA, QS), 1)
    marked = jnp.where(slot < counts[...], lists[...], QB)
    tail = jnp.concatenate([marked, jnp.zeros((NA, AUXB - QS), jnp.int32)], axis=1)
    tail = jnp.concatenate([tail, jnp.zeros((8 - NA, AUXB), jnp.int32)], axis=0)
    out[PART : PART + 8, :] = tail.astype(F32).astype(BF16)


def pack(aux_list, aux_count, metric):
    return pl.pallas_call(
        pack_kernel,
        out_shape=jax.ShapeDtypeStruct((PART + 8, AUXB), BF16),
        in_specs=[VMEM] * 3,
        out_specs=VMEM,
        compiler_params=PARAMS,
        name="pack",
    )(aux_list, aux_count, metric)


def line_kernel(sc_ref, m0, m1, m2, m3, out):
    y = sc_ref[0]
    for k, m in enumerate((m0, m1, m2, m3)):
        at = pl.multiple_of(back(y, k) * PART, 32)
        out[pl.ds(at, PART), :] = m[0:PART, :]
    tail = jnp.concatenate([m0[PART : PART + 8, :].astype(F32), jnp.zeros((8, AUXB), F32)], axis=0)
    out[LIST0:SMALL, :] = tail.astype(BF16)


def line(sc, parts):
    return pl.pallas_call(
        line_kernel,
        out_shape=jax.ShapeDtypeStruct((SMALL, AUXB), BF16),
        in_specs=[SMEM] + [VMEM] * 4,
        out_specs=VMEM,
        compiler_params=PARAMS,
        name="line",
    )(sc, *parts)


def fill(tiles, start, met, lists, row, dense, base):
    for i in range(QS):
        q = lists[row, i]
        at = start + i * BS
        fitted = jnp.dot(tiles[at : at + BS, :], met[q], preferred_element_type=F32)
        cols = pl.ds(pl.multiple_of(q * AUXB, AUXB), AUXB)
        dense[pl.ds(pl.multiple_of(base, BS), BS), cols] = fitted.astype(BF16)


def fill_block(tiles, met, lists, row, dense, base):
    for a in range(NA):
        fill(tiles, a * HALF, met, lists, row + a, dense, base + a * BS)


def read_lists(ref, at):
    return ref[at : at + 8, :].astype(F32).astype(jnp.int32)


def build_kernel(
    sc_ref, t0, t1, t2, t3, z1, z3, p0, p1, p2, p3, s0, s1, s2, s3, dy, dz, met, lv, ls, sem
):
    y, zh = sc_ref[0], sc_ref[1]
    for k, p in enumerate((p0, p1, p2, p3)):
        lv[8 * k : 8 * k + 8, :] = read_lists(p, PART)
    for n, s in ((4, s1), (5, s3)):
        lv[8 * n : 8 * n + 8, :] = read_lists(s, LIST0)
    copy = pltpu.make_async_copy(lv, ls, sem)
    copy.start()
    lines = [s[0:LIST0, :].astype(F32) for s in (s0, s1, s2, s3)]
    for src in range(4):
        k = back(zh, src)
        near = jnp.where(k == 0, lines[0], lines[1])
        far = jnp.where(k == 2, lines[2], lines[3])
        rows = jnp.where(k < 2, near, far)
        for ysrc in range(4):
            for q in range(QB):
                at = ysrc * PART + q * MROWS
                to = (4 * ysrc + src) * MROWS
                met[q, to : to + MROWS, :] = rows[at : at + MROWS, :].astype(BF16)
    dy[...] = jnp.zeros_like(dy)
    dz[...] = jnp.zeros_like(dz)
    copy.wait()
    fill_block(t0, met, ls, 0, dy, y * ROWS)
    mine = dy[pl.ds(pl.multiple_of(y * ROWS, ROWS), ROWS), :]
    dz[pl.ds(pl.multiple_of(zh * ROWS, ROWS), ROWS), :] = mine
    for k, t in ((1, t1), (2, t2), (3, t3)):
        fill_block(t, met, ls, 8 * k, dy, back(y, k) * ROWS)
    for n, k, t in ((4, 1, z1), (5, 3, z3)):
        fill_block(t, met, ls, 8 * n, dz, back(zh, k) * ROWS)


def build(sc, tiles, zs, parts, smalls):
    dense = jax.ShapeDtypeStruct((4 * ROWS, WIDE), BF16)
    return pl.pallas_call(
        build_kernel,
        out_shape=(dense, dense, jax.ShapeDtypeStruct((QB + 1, AUXB, AUXB), BF16)),
        in_specs=[SMEM] + [VMEM] * 14,
        out_specs=(VMEM,) * 3,
        scratch_shapes=[
            pltpu.VMEM((48, 128), jnp.int32),
            pltpu.SMEM((48, 128), jnp.int32),
            pltpu.SemaphoreType.DMA,
        ],
        compiler_params=PARAMS,
        name="build",
    )(sc, *tiles, *zs, *parts, *smalls)


def hold_kernel(tiles, late, out):
    out[...] = tiles[...]


def hold(tiles, late):
    return pl.pallas_call(
        hold_kernel,
        out_shape=jax.ShapeDtypeStruct(tiles.shape, tiles.dtype),
        in_specs=[VMEM] * 2,
        out_specs=VMEM,
        compiler_params=PARAMS,
        name="hold",
    )(tiles, late)


def far_kernel(met, f1, f3, s2, far, lv, ls, sem):
    lv[...] = read_lists(s2, LIST0)
    copy = pltpu.make_async_copy(lv, ls, sem)
    copy.start()
    far[...] = jnp.zeros_like(far)
    copy.wait()
    fill(f1, 0, met, ls, 0, far, 0)
    fill(f3, 0, met, ls, 1, far, BS)


def far_block(met, f1, f3, small):
    return pl.pallas_call(
        far_kernel,
        out_shape=jax.ShapeDtypeStruct((ROWS, WIDE), BF16),
        in_specs=[VMEM] * 4,
        out_specs=VMEM,
        scratch_shapes=[
            pltpu.VMEM((8, 128), jnp.int32),
            pltpu.SMEM((8, 128), jnp.int32),
            pltpu.SemaphoreType.DMA,
        ],
        compiler_params=PARAMS,
        name="far",
    )(met, f1, f3, small)


def gram_kernel(flip, shifts, sc_ref, dy, dz, far, out):
    zh, co, x = sc_ref[1], sc_ref[2], sc_ref[3]
    core = 1 - co if flip else co
    inner = jnp.logical_or(zh == 1, zh == 2)
    opposite = back(zh, 2)
    factor = 1.0 / (QS * 16 * AUXB) ** 0.5
    for h in range(2):
        p = jnp.where(inner, 2 * h + core, h + 2 * core)

        def product(rhs):
            for i, k in enumerate(shifts):
                q = lax.rem(x + k, 4)
                lhs = dy[pl.ds(pl.multiple_of(q * ROWS, ROWS), ROWS), 0:USED]
                prod = lax.dot_general(
                    lhs, rhs, (((1,), (1,)), ((), ())), preferred_element_type=F32
                )
                out[i, h] = prod * factor

        @pl.when(p == opposite)
        def _():
            product(far[:, 0:USED])

        @pl.when(p != opposite)
        def _():
            product(dz[pl.ds(pl.multiple_of(p * ROWS, ROWS), ROWS), 0:USED])


def gram(flip, shifts, sc, dy, dz, far):
    return pl.pallas_call(
        functools.partial(gram_kernel, flip, shifts),
        out_shape=jax.ShapeDtypeStruct((2, 2, ROWS, ROWS), F32),
        in_specs=[SMEM] + [VMEM] * 3,
        out_specs=VMEM,
        compiler_params=PARAMS,
    )(sc, dy, dz, far)


def share_kernel(sc_ref, keep, got, *outs):
    zl = sc_ref[4]
    for n, out in enumerate(outs):
        h = lax.rem(zl + n % 2, 2)
        out[...] = (keep[n // 2, h] + got[n // 2, h]).astype(out.dtype)


def share(sc, keep, got, types):
    return pl.pallas_call(
        share_kernel,
        out_shape=tuple(jax.ShapeDtypeStruct((ROWS, ROWS), t) for t in types),
        in_specs=[SMEM, VMEM, VMEM],
        out_specs=(VMEM,) * 4,
        compiler_params=PARAMS,
        name="share",
    )(sc, keep, got)


def landed(z, zl, co):
    return 2 * zl + co if z in (1, 2) else zl + 2 * co


def hop(k, w):
    return [(2 * a + b, 2 * ((a + k) % 4) + (b + w) % 2) for a in range(4) for b in range(2)]


def local(fit_tiles, aux_list, aux_count, metric):
    sc = jnp.stack([lax.axis_index(n) for n in ("y", "zh", "co", "x", "zl")]).astype(jnp.int32)
    part = pack(aux_list, aux_count, metric.reshape(PART, AUXB))
    parts = [part] + [lax.ppermute(part, "y", ring(4, k)) for k in (1, 2, 3)]
    tiles = fit_tiles.reshape(2 * HALF, AUXB)
    z1 = lax.ppermute(tiles, "zh", ring(4, 1))
    z3 = lax.ppermute(tiles, "zh", ring(4, 3))
    ys = [tiles] + [lax.ppermute(tiles, "y", ring(4, k)) for k in (1, 2, 3)]
    small = line(sc, parts)
    smalls = [small] + [lax.ppermute(small, "zh", ring(4, k)) for k in (1, 2, 3)]
    f1 = lax.ppermute(z1[:HALF], "zh", ring(4, 1))
    f3 = lax.ppermute(z3[HALF:], "zh", ring(4, 3))

    dy, dz, met = build(sc, [hold(tiles, z3)] + ys[1:], [z1, z3], parts, smalls)
    far = far_block(met, f1, f3, smalls[2])
    pieces = {}
    for shifts, last in (((2, 1), BF16), ((3, 0), F32)):
        send = gram(True, shifts, sc, dy, dz, far)
        got = lax.ppermute(send, "co", ring(2, 1))
        keep = gram(False, shifts, sc, dy, dz, far)
        names = [(k, w) for k in shifts for w in range(2)]
        pieces.update(zip(names, share(sc, keep, got, (BF16, BF16, last, BF16))))
    total = pieces[0, 0]
    for k, w in ((2, 1), (2, 0), (1, 1), (1, 0), (3, 1), (3, 0), (0, 1)):
        total = total + lax.ppermute(pieces[k, w], ("x", "zl"), hop(k, w)).astype(F32)
    spots = [(z, zl, co) for z in range(4) for zl in range(2) for co in range(2)]
    move = [(4 * z + 2 * zl + co, 4 * landed(z, zl, co) + z) for z, zl, co in spots]
    return lax.ppermute(total, ("zh", "zl", "co"), move)


def solution(mesh):
    fine = Mesh(mesh.devices.reshape(4, 4, 4, 2, 2), ("y", "zh", "x", "zl", "co"))
    row, col = ("y", "zh"), ("x", "zl", "co")
    placed = (P(row, col, None, None), P(row, col), P(row, col), P(col, row, None))

    return jax.shard_map(local, mesh=fine, in_specs=placed, out_specs=P(col, row), check_vma=False)
```

```python
import functools

import jax
import jax.numpy as jnp
from jax import lax
from jax.experimental import pallas as pl
from jax.experimental.pallas import tpu as pltpu
from jax.sharding import Mesh, PartitionSpec as P


AUXB = 128
BS = 128
QS = 6
QB = 12
NA = 2
ROWS = NA * BS
WIDE = (QB + 1) * AUXB
USED = QB * AUXB
MROWS = 8
HALF = QS * BS
PART = QB * MROWS
LIST0 = 4 * PART
SMALL = LIST0 + 16
F32 = jnp.float32
BF16 = jnp.bfloat16

SMEM = pl.BlockSpec(memory_space=pltpu.SMEM)
VMEM = pl.BlockSpec(memory_space=pltpu.VMEM)
PARAMS = pltpu.CompilerParams(vmem_limit_bytes=14 << 20)


def ring(n, k):
    return [(i, (i + k) % n) for i in range(n)]


def back(i, k):
    return lax.rem(i - k + 4, 4)


def pack_kernel(lists, counts, metric, out):
    out[0:PART, :] = metric[...]
    slot = lax.broadcasted_iota(jnp.int32, (NA, QS), 1)
    marked = jnp.where(slot < counts[...], lists[...], QB)
    tail = jnp.concatenate([marked, jnp.zeros((NA, AUXB - QS), jnp.int32)], axis=1)
    tail = jnp.concatenate([tail, jnp.zeros((8 - NA, AUXB), jnp.int32)], axis=0)
    out[PART : PART + 8, :] = tail.astype(F32).astype(BF16)


def pack(aux_list, aux_count, metric):
    return pl.pallas_call(
        pack_kernel,
        out_shape=jax.ShapeDtypeStruct((PART + 8, AUXB), BF16),
        in_specs=[VMEM] * 3,
        out_specs=VMEM,
        compiler_params=PARAMS,
        name="pack",
    )(aux_list, aux_count, metric)


def line_kernel(sc_ref, m0, m1, m2, m3, out):
    y = sc_ref[0]
    for k, m in enumerate((m0, m1, m2, m3)):
        at = pl.multiple_of(back(y, k) * PART, 32)
        out[pl.ds(at, PART), :] = m[0:PART, :]
    tail = jnp.concatenate([m0[PART : PART + 8, :].astype(F32), jnp.zeros((8, AUXB), F32)], axis=0)
    out[LIST0:SMALL, :] = tail.astype(BF16)


def line(sc, parts):
    return pl.pallas_call(
        line_kernel,
        out_shape=jax.ShapeDtypeStruct((SMALL, AUXB), BF16),
        in_specs=[SMEM] + [VMEM] * 4,
        out_specs=VMEM,
        compiler_params=PARAMS,
        name="line",
    )(sc, *parts)


def fill(tiles, start, met, lists, row, dense, base):
    for i in range(QS):
        q = lists[row, i]
        at = start + i * BS
        fitted = jnp.dot(tiles[at : at + BS, :], met[q], preferred_element_type=F32)
        cols = pl.ds(pl.multiple_of(q * AUXB, AUXB), AUXB)
        dense[pl.ds(pl.multiple_of(base, BS), BS), cols] = fitted.astype(BF16)


def fill_block(tiles, met, lists, row, dense, base):
    for a in range(NA):
        fill(tiles, a * HALF, met, lists, row + a, dense, base + a * BS)


def read_lists(ref, at):
    return ref[at : at + 8, :].astype(F32).astype(jnp.int32)


def build_kernel(
    sc_ref, t0, t1, t2, t3, z1, z3, p0, p1, p2, p3, s0, s1, s2, s3, dy, dz, met, lv, ls, sem
):
    y, zh = sc_ref[0], sc_ref[1]
    for k, p in enumerate((p0, p1, p2, p3)):
        lv[8 * k : 8 * k + 8, :] = read_lists(p, PART)
    for n, s in ((4, s1), (5, s3)):
        lv[8 * n : 8 * n + 8, :] = read_lists(s, LIST0)
    copy = pltpu.make_async_copy(lv, ls, sem)
    copy.start()
    lines = [s[0:LIST0, :].astype(F32) for s in (s0, s1, s2, s3)]
    for src in range(4):
        k = back(zh, src)
        near = jnp.where(k == 0, lines[0], lines[1])
        far = jnp.where(k == 2, lines[2], lines[3])
        rows = jnp.where(k < 2, near, far)
        for ysrc in range(4):
            for q in range(QB):
                at = ysrc * PART + q * MROWS
                to = (4 * ysrc + src) * MROWS
                met[q, to : to + MROWS, :] = rows[at : at + MROWS, :].astype(BF16)
    dy[...] = jnp.zeros_like(dy)
    dz[...] = jnp.zeros_like(dz)
    copy.wait()
    fill_block(t0, met, ls, 0, dy, y * ROWS)
    mine = dy[pl.ds(pl.multiple_of(y * ROWS, ROWS), ROWS), :]
    dz[pl.ds(pl.multiple_of(zh * ROWS, ROWS), ROWS), :] = mine
    for k, t in ((1, t1), (2, t2), (3, t3)):
        fill_block(t, met, ls, 8 * k, dy, back(y, k) * ROWS)
    for n, k, t in ((4, 1, z1), (5, 3, z3)):
        fill_block(t, met, ls, 8 * n, dz, back(zh, k) * ROWS)


def build(sc, tiles, zs, parts, smalls):
    dense = jax.ShapeDtypeStruct((4 * ROWS, WIDE), BF16)
    return pl.pallas_call(
        build_kernel,
        out_shape=(dense, dense, jax.ShapeDtypeStruct((QB + 1, AUXB, AUXB), BF16)),
        in_specs=[SMEM] + [VMEM] * 14,
        out_specs=(VMEM,) * 3,
        scratch_shapes=[
            pltpu.VMEM((48, 128), jnp.int32),
            pltpu.SMEM((48, 128), jnp.int32),
            pltpu.SemaphoreType.DMA,
        ],
        compiler_params=PARAMS,
        name="build",
    )(sc, *tiles, *zs, *parts, *smalls)


def gram_kernel(flip, sc_ref, dy, dz, met, f1, f3, s2, out, far, lv, ls, sem):
    zh, co = sc_ref[1], sc_ref[2]
    parity = 1 - co if flip else co
    opposite = back(zh, 2)
    factor = 1.0 / (QS * 16 * AUXB) ** 0.5

    @pl.when(lax.rem(zh, 2) == parity)
    def _():
        lv[...] = read_lists(s2, LIST0)
        copy = pltpu.make_async_copy(lv, ls, sem)
        copy.start()
        far[...] = jnp.zeros_like(far)
        copy.wait()
        fill(f1, 0, met, ls, 0, far, 0)
        fill(f3, 0, met, ls, 1, far, BS)

    def product(h, swapped, block):
        for q in range(4):
            row = dy[q * ROWS : (q + 1) * ROWS, 0:USED]
            pair = (block, row) if swapped else (row, block)
            prod = lax.dot_general(*pair, (((1,), (1,)), ((), ())), preferred_element_type=F32)
            out[q, h] = prod * factor

    for h in range(2):
        p = 2 * h + parity

        @pl.when(p == opposite)
        def _():
            product(h, True, far[:, 0:USED])

        @pl.when(p != opposite)
        def _():
            at = pl.multiple_of(p * ROWS, ROWS)
            product(h, False, dz[pl.ds(at, ROWS), 0:USED])


def gram(flip, sc, dy, dz, met, f1, f3, small):
    return pl.pallas_call(
        functools.partial(gram_kernel, flip),
        out_shape=jax.ShapeDtypeStruct((4, 2, ROWS, ROWS), F32),
        in_specs=[SMEM] + [VMEM] * 6,
        out_specs=VMEM,
        scratch_shapes=[
            pltpu.VMEM((ROWS, WIDE), BF16),
            pltpu.VMEM((8, 128), jnp.int32),
            pltpu.SMEM((8, 128), jnp.int32),
            pltpu.SemaphoreType.DMA,
        ],
        compiler_params=PARAMS,
        name="send" if flip else "keep",
    )(sc, dy, dz, met, f1, f3, small)


def hold_kernel(tiles, late, out):
    out[...] = tiles[...]


def hold(tiles, late):
    return pl.pallas_call(
        hold_kernel,
        out_shape=jax.ShapeDtypeStruct(tiles.shape, tiles.dtype),
        in_specs=[VMEM] * 2,
        out_specs=VMEM,
        compiler_params=PARAMS,
        name="hold",
    )(tiles, late)


STEPS = tuple((k, w) for w in range(2) for k in range(4))


def share_kernel(sc_ref, keep, got, own, *outs):
    x, zl = sc_ref[3], sc_ref[4]
    for (k, w), out in zip(STEPS, (own,) + outs):
        q, h = lax.rem(x + k, 4), lax.rem(zl + w, 2)
        out[...] = (keep[q, h] + got[q, h]).astype(out.dtype)


def share(sc, keep, got):
    piece = (ROWS, ROWS)
    return pl.pallas_call(
        share_kernel,
        out_shape=(jax.ShapeDtypeStruct(piece, F32),) + (jax.ShapeDtypeStruct(piece, BF16),) * 7,
        in_specs=[SMEM, VMEM, VMEM],
        out_specs=(VMEM,) * 8,
        compiler_params=PARAMS,
        name="share",
    )(sc, keep, got)


def hop(k, w):
    return [(2 * a + b, 2 * ((a + k) % 4) + (b + w) % 2) for a in range(4) for b in range(2)]


def homes():
    moves = []
    for n in range(256):
        y, z, x, p = n // 64, n // 16 % 4, n // 4 % 4, n % 4
        home = (x, z, y, p) if p == (z + 2) % 4 else (y, p, x, z)
        moves.append((n, home[0] * 64 + home[1] * 16 + home[2] * 4 + home[3]))
    return moves


def local(fit_tiles, aux_list, aux_count, metric):
    sc = jnp.stack([lax.axis_index(n) for n in ("y", "zh", "co", "x", "zl")]).astype(jnp.int32)
    part = pack(aux_list, aux_count, metric.reshape(PART, AUXB))
    parts = [part] + [lax.ppermute(part, "y", ring(4, k)) for k in (1, 2, 3)]
    tiles = fit_tiles.reshape(2 * HALF, AUXB)
    z1 = lax.ppermute(tiles, "zh", ring(4, 1))
    z3 = lax.ppermute(tiles, "zh", ring(4, 3))
    ys = [tiles] + [lax.ppermute(tiles, "y", ring(4, k)) for k in (1, 2, 3)]
    small = line(sc, parts)
    smalls = [small] + [lax.ppermute(small, "zh", ring(4, k)) for k in (1, 2, 3)]
    f1 = lax.ppermute(z1[:HALF], "zh", ring(4, 1))
    f3 = lax.ppermute(z3[HALF:], "zh", ring(4, 3))

    dy, dz, met = build(sc, [hold(tiles, z3)] + ys[1:], [z1, z3], parts, smalls)
    send = gram(True, sc, dy, dz, met, f1, f3, smalls[2])
    got = lax.ppermute(send, "co", ring(2, 1))
    keep = gram(False, sc, dy, dz, met, f1, f3, smalls[2])
    total, *shares = share(sc, keep, got)
    for (k, w), piece in zip(STEPS[1:], shares):
        total = total + lax.ppermute(piece, ("x", "zl"), hop(k, w)).astype(F32)
    return lax.ppermute(total, ("y", "zh", "x", "zl", "co"), homes())


def solution(mesh):
    fine = Mesh(mesh.devices.reshape(4, 4, 4, 2, 2), ("y", "zh", "x", "zl", "co"))
    row, col = ("y", "zh"), ("x", "zl", "co")
    placed = (P(row, col, None, None), P(row, col), P(row, col), P(col, row, None))

    return jax.shard_map(local, mesh=fine, in_specs=placed, out_specs=P(col, row), check_vma=False)
```

```python
import jax
import jax.numpy as jnp
from jax import lax
from jax.experimental import pallas as pl
from jax.experimental.pallas import tpu as pltpu
from jax.sharding import Mesh, PartitionSpec as P


AUXB = 128
BS = 128
QS = 6
QB = 12
NA = 2
ROWS = NA * BS
WIDE = (QB + 1) * AUXB
USED = QB * AUXB
MROWS = 8
HALF = QS * BS
PART = QB * MROWS
LIST0 = 4 * PART
SMALL = LIST0 + 16
F32 = jnp.float32
BF16 = jnp.bfloat16

SMEM = pl.BlockSpec(memory_space=pltpu.SMEM)
VMEM = pl.BlockSpec(memory_space=pltpu.VMEM)
PARAMS = pltpu.CompilerParams(vmem_limit_bytes=14 << 20)


def ring(n, k):
    return [(i, (i + k) % n) for i in range(n)]


def back(i, k):
    return lax.rem(i - k + 4, 4)


def pack_kernel(lists, counts, metric, out):
    out[0:PART, :] = metric[...]
    slot = lax.broadcasted_iota(jnp.int32, (NA, QS), 1)
    marked = jnp.where(slot < counts[...], lists[...], QB)
    tail = jnp.concatenate([marked, jnp.zeros((NA, AUXB - QS), jnp.int32)], axis=1)
    tail = jnp.concatenate([tail, jnp.zeros((8 - NA, AUXB), jnp.int32)], axis=0)
    out[PART : PART + 8, :] = tail.astype(F32).astype(BF16)


def pack(aux_list, aux_count, metric):
    return pl.pallas_call(
        pack_kernel,
        out_shape=jax.ShapeDtypeStruct((PART + 8, AUXB), BF16),
        in_specs=[VMEM] * 3,
        out_specs=VMEM,
        compiler_params=PARAMS,
        name="pack",
    )(aux_list, aux_count, metric)


def line_kernel(sc_ref, m0, m1, m2, m3, out):
    y = sc_ref[0]
    for k, m in enumerate((m0, m1, m2, m3)):
        at = pl.multiple_of(back(y, k) * PART, 32)
        out[pl.ds(at, PART), :] = m[0:PART, :]
    tail = jnp.concatenate([m0[PART : PART + 8, :].astype(F32), jnp.zeros((8, AUXB), F32)], axis=0)
    out[LIST0:SMALL, :] = tail.astype(BF16)


def line(sc, parts):
    return pl.pallas_call(
        line_kernel,
        out_shape=jax.ShapeDtypeStruct((SMALL, AUXB), BF16),
        in_specs=[SMEM] + [VMEM] * 4,
        out_specs=VMEM,
        compiler_params=PARAMS,
        name="line",
    )(sc, *parts)


def fill(tiles, start, met, lists, row, dense, base):
    for i in range(QS):
        q = lists[row, i]
        at = start + i * BS
        fitted = jnp.dot(tiles[at : at + BS, :], met[q], preferred_element_type=F32)
        cols = pl.ds(pl.multiple_of(q * AUXB, AUXB), AUXB)
        dense[pl.ds(pl.multiple_of(base, BS), BS), cols] = fitted.astype(BF16)


def fill_block(tiles, met, lists, row, dense, base):
    for a in range(NA):
        fill(tiles, a * HALF, met, lists, row + a, dense, base + a * BS)


def read_lists(ref, at):
    return ref[at : at + 8, :].astype(F32).astype(jnp.int32)


def build_kernel(
    sc_ref, t0, t1, t2, t3, z1, z3, p0, p1, p2, p3, s0, s1, s2, s3, dy, dz, met, lv, ls, sem
):
    y, zh = sc_ref[0], sc_ref[1]
    for k, p in enumerate((p0, p1, p2, p3)):
        lv[8 * k : 8 * k + 8, :] = read_lists(p, PART)
    for n, s in ((4, s1), (5, s3)):
        lv[8 * n : 8 * n + 8, :] = read_lists(s, LIST0)
    copy = pltpu.make_async_copy(lv, ls, sem)
    copy.start()
    lines = [s[0:LIST0, :].astype(F32) for s in (s0, s1, s2, s3)]
    for src in range(4):
        k = back(zh, src)
        near = jnp.where(k == 0, lines[0], lines[1])
        far = jnp.where(k == 2, lines[2], lines[3])
        rows = jnp.where(k < 2, near, far)
        for ysrc in range(4):
            for q in range(QB):
                at = ysrc * PART + q * MROWS
                to = (4 * ysrc + src) * MROWS
                met[q, to : to + MROWS, :] = rows[at : at + MROWS, :].astype(BF16)
    dy[...] = jnp.zeros_like(dy)
    dz[...] = jnp.zeros_like(dz)
    copy.wait()
    fill_block(t0, met, ls, 0, dy, y * ROWS)
    mine = dy[pl.ds(pl.multiple_of(y * ROWS, ROWS), ROWS), :]
    dz[pl.ds(pl.multiple_of(zh * ROWS, ROWS), ROWS), :] = mine
    for k, t in ((1, t1), (2, t2), (3, t3)):
        fill_block(t, met, ls, 8 * k, dy, back(y, k) * ROWS)
    for n, k, t in ((4, 1, z1), (5, 3, z3)):
        fill_block(t, met, ls, 8 * n, dz, back(zh, k) * ROWS)


def build(sc, tiles, zs, parts, smalls):
    dense = jax.ShapeDtypeStruct((4 * ROWS, WIDE), BF16)
    return pl.pallas_call(
        build_kernel,
        out_shape=(dense, dense, jax.ShapeDtypeStruct((QB + 1, AUXB, AUXB), BF16)),
        in_specs=[SMEM] + [VMEM] * 14,
        out_specs=(VMEM,) * 3,
        scratch_shapes=[
            pltpu.VMEM((48, 128), jnp.int32),
            pltpu.SMEM((48, 128), jnp.int32),
            pltpu.SemaphoreType.DMA,
        ],
        compiler_params=PARAMS,
        name="build",
    )(sc, *tiles, *zs, *parts, *smalls)


FACTOR = 1.0 / (QS * 16 * AUXB) ** 0.5


def early(zh, core):
    opposite = back(zh, 2)
    return jnp.where(lax.rem(zh, 2) == core, 1 - opposite // 2, 0)


def product(out, dy, block, swapped):
    for q in range(4):
        row = dy[q * ROWS : (q + 1) * ROWS, 0:USED]
        pair = (block, row) if swapped else (row, block)
        prod = lax.dot_general(*pair, (((1,), (1,)), ((), ())), preferred_element_type=F32)
        out[q] = prod * FACTOR


def near_product(out, dy, dz, h, core):
    at = pl.multiple_of((2 * h + core) * ROWS, ROWS)
    product(out, dy, dz[pl.ds(at, ROWS), 0:USED], False)


def first_kernel(sc_ref, dy, dz, send_e):
    zh, other = sc_ref[1], 1 - sc_ref[2]
    near_product(send_e, dy, dz, early(zh, other), other)


def near_kernel(sc_ref, dy, dz, keep_e, send_l, keep_l):
    zh, co = sc_ref[1], sc_ref[2]
    near_product(keep_e, dy, dz, early(zh, co), co)
    mine = lax.rem(zh, 2) == co

    @pl.when(mine)
    def _():
        near_product(send_l, dy, dz, 1 - early(zh, 1 - co), 1 - co)

    @pl.when(jnp.logical_not(mine))
    def _():
        near_product(keep_l, dy, dz, 1 - early(zh, co), co)


def far_kernel(sc_ref, dy, met, f1, f3, s2, send_in, keep_in, send_l, keep_l, far, lv, ls, sem):
    lv[...] = read_lists(s2, LIST0)
    copy = pltpu.make_async_copy(lv, ls, sem)
    copy.start()
    far[...] = jnp.zeros_like(far)
    copy.wait()
    fill(f1, 0, met, ls, 0, far, 0)
    fill(f3, 0, met, ls, 1, far, BS)
    mine = lax.rem(sc_ref[1], 2) == sc_ref[2]
    pl.when(mine)(lambda: product(keep_l, dy, far[:, 0:USED], True))
    pl.when(jnp.logical_not(mine))(lambda: product(send_l, dy, far[:, 0:USED], True))


ROW = jax.ShapeDtypeStruct((4, ROWS, ROWS), F32)


def first_row(sc, dy, dz):
    return pl.pallas_call(
        first_kernel,
        out_shape=ROW,
        in_specs=[SMEM, VMEM, VMEM],
        out_specs=VMEM,
        compiler_params=PARAMS,
        name="first",
    )(sc, dy, dz)


def near_rows(sc, dy, dz):
    return pl.pallas_call(
        near_kernel,
        out_shape=(ROW,) * 3,
        in_specs=[SMEM, VMEM, VMEM],
        out_specs=(VMEM,) * 3,
        compiler_params=PARAMS,
        name="near",
    )(sc, dy, dz)


def far_row(sc, dy, met, f1, f3, small, send_l, keep_l):
    return pl.pallas_call(
        far_kernel,
        out_shape=(ROW,) * 2,
        in_specs=[SMEM] + [VMEM] * 7,
        out_specs=(VMEM,) * 2,
        scratch_shapes=[
            pltpu.VMEM((ROWS, WIDE), BF16),
            pltpu.VMEM((8, 128), jnp.int32),
            pltpu.SMEM((8, 128), jnp.int32),
            pltpu.SemaphoreType.DMA,
        ],
        input_output_aliases={6: 0, 7: 1},
        compiler_params=PARAMS,
        name="far",
    )(sc, dy, met, f1, f3, small, send_l, keep_l)


def hold_kernel(tiles, late, out):
    out[...] = tiles[...]


def hold(tiles, late):
    return pl.pallas_call(
        hold_kernel,
        out_shape=jax.ShapeDtypeStruct(tiles.shape, tiles.dtype),
        in_specs=[VMEM] * 2,
        out_specs=VMEM,
        compiler_params=PARAMS,
        name="hold",
    )(tiles, late)


STEPS = tuple((k, w) for w in range(2) for k in range(4))


def share_kernel(sc_ref, keep_e, got_e, keep_l, got_l, *outs):
    zh, co, x, zl = sc_ref[1], sc_ref[2], sc_ref[3], sc_ref[4]

    def write(order):
        for (k, w), out in zip(STEPS, outs):
            q = lax.rem(x + k, 4)
            keep, got = order[w]
            out[...] = (keep[q] + got[q]).astype(out.dtype)

    rows = ((keep_e, got_e), (keep_l, got_l))
    same = early(zh, co) == zl
    pl.when(same)(lambda: write(rows))
    pl.when(jnp.logical_not(same))(lambda: write(rows[::-1]))


def share(sc, *rows):
    piece = (ROWS, ROWS)
    return pl.pallas_call(
        share_kernel,
        out_shape=(jax.ShapeDtypeStruct(piece, F32),) + (jax.ShapeDtypeStruct(piece, BF16),) * 7,
        in_specs=[SMEM] + [VMEM] * 4,
        out_specs=(VMEM,) * 8,
        compiler_params=PARAMS,
        name="share",
    )(sc, *rows)


def hop(k, w):
    return [(2 * a + b, 2 * ((a + k) % 4) + (b + w) % 2) for a in range(4) for b in range(2)]


def homes():
    moves = []
    for n in range(256):
        y, z, x, p = n // 64, n // 16 % 4, n // 4 % 4, n % 4
        home = (x, z, y, p) if p == (z + 2) % 4 else (y, p, x, z)
        moves.append((n, home[0] * 64 + home[1] * 16 + home[2] * 4 + home[3]))
    return moves


def local(fit_tiles, aux_list, aux_count, metric):
    sc = jnp.stack([lax.axis_index(n) for n in ("y", "zh", "co", "x", "zl")]).astype(jnp.int32)
    part = pack(aux_list, aux_count, metric.reshape(PART, AUXB))
    parts = [part] + [lax.ppermute(part, "y", ring(4, k)) for k in (1, 2, 3)]
    tiles = fit_tiles.reshape(2 * HALF, AUXB)
    z1 = lax.ppermute(tiles, "zh", ring(4, 1))
    z3 = lax.ppermute(tiles, "zh", ring(4, 3))
    ys = [tiles] + [lax.ppermute(tiles, "y", ring(4, k)) for k in (1, 2, 3)]
    small = line(sc, parts)
    smalls = [small] + [lax.ppermute(small, "zh", ring(4, k)) for k in (1, 2, 3)]
    f1 = lax.ppermute(z1[:HALF], "zh", ring(4, 1))
    f3 = lax.ppermute(z3[HALF:], "zh", ring(4, 3))

    dy, dz, met = build(sc, [hold(tiles, z3)] + ys[1:], [z1, z3], parts, smalls)
    got_e = lax.ppermute(first_row(sc, dy, dz), "co", ring(2, 1))
    keep_e, send_l, keep_l = near_rows(sc, dy, dz)
    send_l, keep_l = far_row(sc, dy, met, f1, f3, smalls[2], send_l, keep_l)
    got_l = lax.ppermute(send_l, "co", ring(2, 1))
    total, *shares = share(sc, keep_e, got_e, keep_l, got_l)
    for (k, w), piece in zip(STEPS[1:], shares):
        total = total + lax.ppermute(piece, ("x", "zl"), hop(k, w)).astype(F32)
    return lax.ppermute(total, ("y", "zh", "x", "zl", "co"), homes())


def solution(mesh):
    fine = Mesh(mesh.devices.reshape(4, 4, 4, 2, 2), ("y", "zh", "x", "zl", "co"))
    row, col = ("y", "zh"), ("x", "zl", "co")
    placed = (P(row, col, None, None), P(row, col), P(row, col), P(col, row, None))

    return jax.shard_map(local, mesh=fine, in_specs=placed, out_specs=P(col, row), check_vma=False)
```

```python
import functools

import jax
import jax.numpy as jnp
from jax import lax
from jax.experimental import pallas as pl
from jax.experimental.pallas import tpu as pltpu
from jax.sharding import Mesh, PartitionSpec as P


AUXB = 128
BS = 128
QS = 6
QB = 12
NA = 2
ROWS = NA * BS
WIDE = (QB + 1) * AUXB
USED = QB * AUXB
MROWS = 8
HALF = QS * BS
PART = QB * MROWS
LIST0 = 4 * PART
SMALL = LIST0 + 16
MHALF = LIST0 // 2
F32 = jnp.float32
BF16 = jnp.bfloat16

SMEM = pl.BlockSpec(memory_space=pltpu.SMEM)
VMEM = pl.BlockSpec(memory_space=pltpu.VMEM)
PARAMS = pltpu.CompilerParams(vmem_limit_bytes=14 << 20)


def ring(n, k):
    return [(i, (i + k) % n) for i in range(n)]


def back(i, k):
    return lax.rem(i - k + 4, 4)


def pack_kernel(lists, counts, metric, out):
    out[0:PART, :] = metric[...]
    slot = lax.broadcasted_iota(jnp.int32, (NA, QS), 1)
    marked = jnp.where(slot < counts[...], lists[...], QB)
    tail = jnp.concatenate([marked, jnp.zeros((NA, AUXB - QS), jnp.int32)], axis=1)
    tail = jnp.concatenate([tail, jnp.zeros((8 - NA, AUXB), jnp.int32)], axis=0)
    out[PART : PART + 8, :] = tail.astype(F32).astype(BF16)


def pack(aux_list, aux_count, metric):
    return pl.pallas_call(
        pack_kernel,
        out_shape=jax.ShapeDtypeStruct((PART + 8, AUXB), BF16),
        in_specs=[VMEM] * 3,
        out_specs=VMEM,
        compiler_params=PARAMS,
        name="pack",
    )(aux_list, aux_count, metric)


def line_kernel(sc_ref, m0, m1, m2, m3, out):
    y = sc_ref[0]
    for k, m in enumerate((m0, m1, m2, m3)):
        at = pl.multiple_of(back(y, k) * PART, 32)
        out[pl.ds(at, PART), :] = m[0:PART, :]
    tail = jnp.concatenate([m0[PART : PART + 8, :].astype(F32), jnp.zeros((8, AUXB), F32)], axis=0)
    out[LIST0:SMALL, :] = tail.astype(BF16)


def line(sc, parts):
    return pl.pallas_call(
        line_kernel,
        out_shape=jax.ShapeDtypeStruct((SMALL, AUXB), BF16),
        in_specs=[SMEM] + [VMEM] * 4,
        out_specs=VMEM,
        compiler_params=PARAMS,
        name="line",
    )(sc, *parts)


def fill(tiles, start, met, lists, row, dense, base):
    for i in range(QS):
        q = lists[row, i]
        at = start + i * BS
        fitted = jnp.dot(tiles[at : at + BS, :], met[q], preferred_element_type=F32)
        cols = pl.ds(pl.multiple_of(q * AUXB, AUXB), AUXB)
        dense[pl.ds(pl.multiple_of(base, BS), BS), cols] = fitted.astype(BF16)


def fill_block(tiles, met, lists, row, dense, base):
    for a in range(NA):
        fill(tiles, a * HALF, met, lists, row + a, dense, base + a * BS)


def read_lists(ref, at):
    return ref[at : at + 8, :].astype(F32).astype(jnp.int32)


def relay_kernel(first, tiles, rows, out):
    start, at = (0, 0) if first else (HALF, MHALF)
    out[0:HALF, :] = tiles[start : start + HALF, :]
    out[HALF : out.shape[0], :] = rows[at : at + out.shape[0] - HALF, :]


def relay(first, tiles, rows):
    size = HALF + (MHALF if first else SMALL - MHALF)
    return pl.pallas_call(
        functools.partial(relay_kernel, first),
        out_shape=jax.ShapeDtypeStruct((size, AUXB), BF16),
        in_specs=[VMEM] * 2,
        out_specs=VMEM,
        compiler_params=PARAMS,
        name="relay",
    )(tiles, rows)


def build_kernel(
    sc_ref, t0, t1, t2, t3, z1, z3, f1, f3, p0, p1, p2, p3, s0, s1, s3, dy, dz, met, lv, ls, sem
):
    y, zh = sc_ref[0], sc_ref[1]
    for k, p in enumerate((p0, p1, p2, p3)):
        lv[8 * k : 8 * k + 8, :] = read_lists(p, PART)
    for n, s, at in ((4, s1, LIST0), (5, s3, LIST0), (6, f3, HALF + MHALF)):
        lv[8 * n : 8 * n + 8, :] = read_lists(s, at)
    copy = pltpu.make_async_copy(lv, ls, sem)
    copy.start()
    two = [f[HALF : HALF + MHALF, :].astype(F32) for f in (f1, f3)]
    lines = [s[0:LIST0, :].astype(F32) for s in (s0, s1, s3)]
    lines.insert(2, jnp.concatenate(two, axis=0))
    for src in range(4):
        k = back(zh, src)
        near = jnp.where(k == 0, lines[0], lines[1])
        far = jnp.where(k == 2, lines[2], lines[3])
        rows = jnp.where(k < 2, near, far)
        for ysrc in range(4):
            for q in range(QB):
                at = ysrc * PART + q * MROWS
                to = (4 * ysrc + src) * MROWS
                met[q, to : to + MROWS, :] = rows[at : at + MROWS, :].astype(BF16)
    dy[...] = jnp.zeros_like(dy)
    dz[...] = jnp.zeros_like(dz)
    copy.wait()
    fill_block(t0, met, ls, 0, dy, y * ROWS)
    mine = dy[pl.ds(pl.multiple_of(y * ROWS, ROWS), ROWS), :]
    dz[pl.ds(pl.multiple_of(zh * ROWS, ROWS), ROWS), :] = mine
    for k, t in ((1, t1), (2, t2), (3, t3)):
        fill_block(t, met, ls, 8 * k, dy, back(y, k) * ROWS)
    for n, k, t in ((4, 1, z1), (5, 3, z3)):
        fill_block(t, met, ls, 8 * n, dz, back(zh, k) * ROWS)
    for a, f in enumerate((f1, f3)):
        fill(f, 0, met, ls, 48 + a, dz, back(zh, 2) * ROWS + a * BS)


def build(sc, tiles, zs, parts, smalls):
    dense = jax.ShapeDtypeStruct((4 * ROWS, WIDE), BF16)
    return pl.pallas_call(
        build_kernel,
        out_shape=(dense, dense),
        in_specs=[SMEM] + [VMEM] * 15,
        out_specs=(VMEM,) * 2,
        scratch_shapes=[
            pltpu.VMEM((QB + 1, AUXB, AUXB), BF16),
            pltpu.VMEM((56, 128), jnp.int32),
            pltpu.SMEM((56, 128), jnp.int32),
            pltpu.SemaphoreType.DMA,
        ],
        compiler_params=PARAMS,
        name="build",
    )(sc, *tiles, *zs, *parts, *smalls)


def gram_kernel(flip, sc_ref, dy, dz, out):
    zh, co = sc_ref[1], sc_ref[2]
    parity = 1 - co if flip else co
    opposite = back(zh, 2)
    factor = 1.0 / (QS * 16 * AUXB) ** 0.5
    for h in range(2):
        p = 2 * h + parity
        block = dz[pl.ds(pl.multiple_of(p * ROWS, ROWS), ROWS), 0:USED]

        def product(swapped):
            for q in range(4):
                row = dy[q * ROWS : (q + 1) * ROWS, 0:USED]
                pair = (block, row) if swapped else (row, block)
                prod = lax.dot_general(*pair, (((1,), (1,)), ((), ())), preferred_element_type=F32)
                out[q, h] = prod * factor

        pl.when(p == opposite)(lambda: product(True))
        pl.when(p != opposite)(lambda: product(False))


def gram(flip, sc, dy, dz):
    return pl.pallas_call(
        functools.partial(gram_kernel, flip),
        out_shape=jax.ShapeDtypeStruct((4, 2, ROWS, ROWS), F32),
        in_specs=[SMEM] + [VMEM] * 2,
        out_specs=VMEM,
        compiler_params=PARAMS,
        name="send" if flip else "keep",
    )(sc, dy, dz)


def hold_kernel(tiles, late, out):
    out[...] = tiles[...]


def hold(tiles, late):
    return pl.pallas_call(
        hold_kernel,
        out_shape=jax.ShapeDtypeStruct(tiles.shape, tiles.dtype),
        in_specs=[VMEM] * 2,
        out_specs=VMEM,
        compiler_params=PARAMS,
        name="hold",
    )(tiles, late)


STEPS = tuple((k, w) for w in range(2) for k in range(4))


def share_kernel(sc_ref, keep, got, own, *outs):
    x, zl = sc_ref[3], sc_ref[4]
    for (k, w), out in zip(STEPS, (own,) + outs):
        q, h = lax.rem(x + k, 4), lax.rem(zl + w, 2)
        out[...] = (keep[q, h] + got[q, h]).astype(out.dtype)


def share(sc, keep, got):
    piece = (ROWS, ROWS)
    return pl.pallas_call(
        share_kernel,
        out_shape=(jax.ShapeDtypeStruct(piece, F32),) + (jax.ShapeDtypeStruct(piece, BF16),) * 7,
        in_specs=[SMEM, VMEM, VMEM],
        out_specs=(VMEM,) * 8,
        compiler_params=PARAMS,
        name="share",
    )(sc, keep, got)


def hop(k, w):
    return [(2 * a + b, 2 * ((a + k) % 4) + (b + w) % 2) for a in range(4) for b in range(2)]


def homes():
    moves = []
    for n in range(256):
        y, z, x, p = n // 64, n // 16 % 4, n // 4 % 4, n % 4
        home = (x, z, y, p) if p == (z + 2) % 4 else (y, p, x, z)
        moves.append((n, home[0] * 64 + home[1] * 16 + home[2] * 4 + home[3]))
    return moves


def local(fit_tiles, aux_list, aux_count, metric):
    sc = jnp.stack([lax.axis_index(n) for n in ("y", "zh", "co", "x", "zl")]).astype(jnp.int32)
    part = pack(aux_list, aux_count, metric.reshape(PART, AUXB))
    parts = [part] + [lax.ppermute(part, "y", ring(4, k)) for k in (1, 2, 3)]
    tiles = fit_tiles.reshape(2 * HALF, AUXB)
    z1 = lax.ppermute(tiles, "zh", ring(4, 1))
    z3 = lax.ppermute(tiles, "zh", ring(4, 3))
    ys = [tiles] + [lax.ppermute(tiles, "y", ring(4, k)) for k in (1, 2, 3)]
    small = line(sc, parts)
    s1 = lax.ppermute(small, "zh", ring(4, 1))
    s3 = lax.ppermute(small, "zh", ring(4, 3))
    f1 = lax.ppermute(relay(True, z1, s1), "zh", ring(4, 1))
    f3 = lax.ppermute(relay(False, z3, s3), "zh", ring(4, 3))

    mine = hold(tiles, z3)
    dy, dz = build(sc, [mine] + ys[1:], [z1, z3, f1, f3], parts, [small, s1, s3])
    send = gram(True, sc, dy, dz)
    got = lax.ppermute(send, "co", ring(2, 1))
    keep = gram(False, sc, dy, dz)
    total, *shares = share(sc, keep, got)
    for (k, w), piece in zip(STEPS[1:], shares):
        total = total + lax.ppermute(piece, ("x", "zl"), hop(k, w)).astype(F32)
    return lax.ppermute(total, ("y", "zh", "x", "zl", "co"), homes())


def solution(mesh):
    fine = Mesh(mesh.devices.reshape(4, 4, 4, 2, 2), ("y", "zh", "x", "zl", "co"))
    row, col = ("y", "zh"), ("x", "zl", "co")
    placed = (P(row, col, None, None), P(row, col), P(row, col), P(col, row, None))

    return jax.shard_map(local, mesh=fine, in_specs=placed, out_specs=P(col, row), check_vma=False)
```

```python
import functools

import jax
import jax.numpy as jnp
from jax import lax
from jax.experimental import pallas as pl
from jax.experimental.pallas import tpu as pltpu
from jax.sharding import Mesh, PartitionSpec as P


AUXB = 128
BS = 128
QS = 6
QB = 12
NA = 2
ROWS = NA * BS
WIDE = (QB + 1) * AUXB
USED = QB * AUXB
MROWS = 8
HALF = QS * BS
PART = QB * MROWS
LIST0 = 4 * PART
SMALL = LIST0 + 16
F32 = jnp.float32
BF16 = jnp.bfloat16

SMEM = pl.BlockSpec(memory_space=pltpu.SMEM)
VMEM = pl.BlockSpec(memory_space=pltpu.VMEM)
PARAMS = pltpu.CompilerParams(vmem_limit_bytes=14 << 20)


def ring(n, k):
    return [(i, (i + k) % n) for i in range(n)]


def back(i, k):
    return lax.rem(i - k + 4, 4)


def pack_kernel(lists, counts, metric, out):
    out[0:PART, :] = metric[...]
    slot = lax.broadcasted_iota(jnp.int32, (NA, QS), 1)
    marked = jnp.where(slot < counts[...], lists[...], QB)
    tail = jnp.concatenate([marked, jnp.zeros((NA, AUXB - QS), jnp.int32)], axis=1)
    tail = jnp.concatenate([tail, jnp.zeros((8 - NA, AUXB), jnp.int32)], axis=0)
    out[PART : PART + 8, :] = tail.astype(F32).astype(BF16)


def pack(aux_list, aux_count, metric):
    return pl.pallas_call(
        pack_kernel,
        out_shape=jax.ShapeDtypeStruct((PART + 8, AUXB), BF16),
        in_specs=[VMEM] * 3,
        out_specs=VMEM,
        compiler_params=PARAMS,
        name="pack",
    )(aux_list, aux_count, metric)


def line_kernel(sc_ref, m0, m1, m2, m3, out):
    zh = sc_ref[1]
    parts = [m[...].astype(F32) for m in (m0, m1, m2, m3)]
    rows = lax.broadcasted_iota(jnp.int32, (8, AUXB), 0)
    tail = jnp.zeros((8, AUXB), F32)
    for src in range(4):
        k = back(zh, src)
        near = jnp.where(k == 0, parts[0], parts[1])
        far = jnp.where(k == 2, parts[2], parts[3])
        part = jnp.where(k < 2, near, far)
        for q in range(QB):
            at = (4 * q + src) * MROWS
            out[at : at + MROWS, :] = part[q * MROWS : (q + 1) * MROWS, :].astype(BF16)
        for a in range(NA):
            tail = jnp.where(rows == NA * src + a, part[PART + a : PART + a + 1, :], tail)
    both = jnp.concatenate([tail, parts[0][PART : PART + 8, :]], axis=0)
    out[LIST0:SMALL, :] = both.astype(BF16)


def line(sc, parts):
    return pl.pallas_call(
        line_kernel,
        out_shape=jax.ShapeDtypeStruct((SMALL, AUXB), BF16),
        in_specs=[SMEM] + [VMEM] * 4,
        out_specs=VMEM,
        compiler_params=PARAMS,
        name="line",
    )(sc, *parts)


def fill(tiles, start, met, lists, row, dense, base):
    for i in range(QS):
        q = lists[row, i]
        at = start + i * BS
        fitted = jnp.dot(tiles[at : at + BS, :], met[q], preferred_element_type=F32)
        cols = pl.ds(pl.multiple_of(q * AUXB, AUXB), AUXB)
        dense[pl.ds(pl.multiple_of(base, BS), BS), cols] = fitted.astype(BF16)


def fill_block(tiles, met, lists, row, dense, base):
    for a in range(NA):
        fill(tiles, a * HALF, met, lists, row + a, dense, base + a * BS)


def read_lists(small):
    return small[LIST0:SMALL, :].astype(F32).astype(jnp.int32)


def build_kernel(sc_ref, t0, t1, t2, t3, z1, z3, s0, s1, s2, s3, dy, dz, met, lv, ls, sem):
    y, zh = sc_ref[0], sc_ref[1]
    for k, s in enumerate((s0, s1, s2, s3)):
        lv[16 * k : 16 * k + 16, :] = read_lists(s)
    copy = pltpu.make_async_copy(lv, ls, sem)
    copy.start()
    for k, s in enumerate((s0, s1, s2, s3)):
        at = pl.multiple_of(back(y, k) * 4 * MROWS, 4 * MROWS)
        met[0:QB, pl.ds(at, 4 * MROWS), :] = s[0:LIST0, :].reshape(QB, 4 * MROWS, AUXB)
    dy[...] = jnp.zeros_like(dy)
    dz[...] = jnp.zeros_like(dz)
    copy.wait()
    fill_block(t0, met, ls, 8, dy, y * ROWS)
    mine = dy[pl.ds(pl.multiple_of(y * ROWS, ROWS), ROWS), :]
    dz[pl.ds(pl.multiple_of(zh * ROWS, ROWS), ROWS), :] = mine
    for k, t in ((1, t1), (2, t2), (3, t3)):
        fill_block(t, met, ls, 16 * k + 8, dy, back(y, k) * ROWS)
    for k, t in ((1, z1), (3, z3)):
        src = back(zh, k)
        fill_block(t, met, ls, NA * src, dz, src * ROWS)


def build(sc, tiles, zs, smalls):
    dense = jax.ShapeDtypeStruct((4 * ROWS, WIDE), BF16)
    return pl.pallas_call(
        build_kernel,
        out_shape=(dense, dense, jax.ShapeDtypeStruct((QB + 1, AUXB, AUXB), BF16)),
        in_specs=[SMEM] + [VMEM] * 10,
        out_specs=(VMEM,) * 3,
        scratch_shapes=[
            pltpu.VMEM((64, 128), jnp.int32),
            pltpu.SMEM((64, 128), jnp.int32),
            pltpu.SemaphoreType.DMA,
        ],
        compiler_params=PARAMS,
        name="build",
    )(sc, *tiles, *zs, *smalls)


def gram_kernel(flip, sc_ref, dy, dz, met, f1, f3, s0, out, far, lv, ls, sem):
    zh, co = sc_ref[1], sc_ref[2]
    parity = 1 - co if flip else co
    opposite = back(zh, 2)
    factor = 1.0 / (QS * 16 * AUXB) ** 0.5

    @pl.when(lax.rem(zh, 2) == parity)
    def _():
        lv[...] = read_lists(s0)
        copy = pltpu.make_async_copy(lv, ls, sem)
        copy.start()
        far[...] = jnp.zeros_like(far)
        copy.wait()
        fill(f1, 0, met, ls, NA * opposite, far, 0)
        fill(f3, 0, met, ls, NA * opposite + 1, far, BS)

    def product(h, swapped, block):
        for q in range(4):
            row = dy[q * ROWS : (q + 1) * ROWS, 0:USED]
            pair = (block, row) if swapped else (row, block)
            prod = lax.dot_general(*pair, (((1,), (1,)), ((), ())), preferred_element_type=F32)
            out[q, h] = prod * factor

    for h in range(2):
        p = 2 * h + parity

        @pl.when(p == opposite)
        def _():
            product(h, True, far[:, 0:USED])

        @pl.when(p != opposite)
        def _():
            at = pl.multiple_of(p * ROWS, ROWS)
            product(h, False, dz[pl.ds(at, ROWS), 0:USED])


def gram(flip, sc, dy, dz, met, f1, f3, small):
    return pl.pallas_call(
        functools.partial(gram_kernel, flip),
        out_shape=jax.ShapeDtypeStruct((4, 2, ROWS, ROWS), F32),
        in_specs=[SMEM] + [VMEM] * 6,
        out_specs=VMEM,
        scratch_shapes=[
            pltpu.VMEM((ROWS, WIDE), BF16),
            pltpu.VMEM((16, 128), jnp.int32),
            pltpu.SMEM((16, 128), jnp.int32),
            pltpu.SemaphoreType.DMA,
        ],
        compiler_params=PARAMS,
        name="send" if flip else "keep",
    )(sc, dy, dz, met, f1, f3, small)


def hold_kernel(tiles, late, out):
    out[...] = tiles[...]


def hold(tiles, late):
    return pl.pallas_call(
        hold_kernel,
        out_shape=jax.ShapeDtypeStruct(tiles.shape, tiles.dtype),
        in_specs=[VMEM] * 2,
        out_specs=VMEM,
        compiler_params=PARAMS,
        name="hold",
    )(tiles, late)


STEPS = tuple((k, w) for w in range(2) for k in range(4))


def share_kernel(sc_ref, keep, got, own, *outs):
    x, zl = sc_ref[3], sc_ref[4]
    for (k, w), out in zip(STEPS, (own,) + outs):
        q, h = lax.rem(x + k, 4), lax.rem(zl + w, 2)
        out[...] = (keep[q, h] + got[q, h]).astype(out.dtype)


def share(sc, keep, got):
    piece = (ROWS, ROWS)
    return pl.pallas_call(
        share_kernel,
        out_shape=(jax.ShapeDtypeStruct(piece, F32),) + (jax.ShapeDtypeStruct(piece, BF16),) * 7,
        in_specs=[SMEM, VMEM, VMEM],
        out_specs=(VMEM,) * 8,
        compiler_params=PARAMS,
        name="share",
    )(sc, keep, got)


def hop(k, w):
    return [(2 * a + b, 2 * ((a + k) % 4) + (b + w) % 2) for a in range(4) for b in range(2)]


def homes():
    moves = []
    for n in range(256):
        y, z, x, p = n // 64, n // 16 % 4, n // 4 % 4, n % 4
        home = (x, z, y, p) if p == (z + 2) % 4 else (y, p, x, z)
        moves.append((n, home[0] * 64 + home[1] * 16 + home[2] * 4 + home[3]))
    return moves


def local(fit_tiles, aux_list, aux_count, metric):
    sc = jnp.stack([lax.axis_index(n) for n in ("y", "zh", "co", "x", "zl")]).astype(jnp.int32)
    part = pack(aux_list, aux_count, metric.reshape(PART, AUXB))
    parts = [part] + [lax.ppermute(part, "zh", ring(4, k)) for k in (1, 2, 3)]
    tiles = fit_tiles.reshape(2 * HALF, AUXB)
    z1 = lax.ppermute(tiles, "zh", ring(4, 1))
    z3 = lax.ppermute(tiles, "zh", ring(4, 3))
    ys = [tiles] + [lax.ppermute(tiles, "y", ring(4, k)) for k in (1, 2, 3)]
    small = line(sc, parts)
    smalls = [small] + [lax.ppermute(small, "y", ring(4, k)) for k in (1, 2, 3)]
    f1 = lax.ppermute(z1[:HALF], "zh", ring(4, 1))
    f3 = lax.ppermute(z3[HALF:], "zh", ring(4, 3))

    dy, dz, met = build(sc, [hold(tiles, z3)] + ys[1:], [z1, z3], smalls)
    send = gram(True, sc, dy, dz, met, f1, f3, small)
    got = lax.ppermute(send, "co", ring(2, 1))
    keep = gram(False, sc, dy, dz, met, f1, f3, small)
    total, *shares = share(sc, keep, got)
    for (k, w), piece in zip(STEPS[1:], shares):
        total = total + lax.ppermute(piece, ("x", "zl"), hop(k, w)).astype(F32)
    return lax.ppermute(total, ("y", "zh", "x", "zl", "co"), homes())


def solution(mesh):
    fine = Mesh(mesh.devices.reshape(4, 4, 4, 2, 2), ("y", "zh", "x", "zl", "co"))
    row, col = ("y", "zh"), ("x", "zl", "co")
    placed = (P(row, col, None, None), P(row, col), P(row, col), P(col, row, None))

    return jax.shard_map(local, mesh=fine, in_specs=placed, out_specs=P(col, row), check_vma=False)
```

```python
import functools

import jax
import jax.numpy as jnp
from jax import lax
from jax.experimental import pallas as pl
from jax.experimental.pallas import tpu as pltpu
from jax.sharding import Mesh, PartitionSpec as P


AUXB = 128
BS = 128
QS = 6
QB = 12
NA = 2
ROWS = NA * BS
WIDE = (QB + 1) * AUXB
USED = QB * AUXB
MROWS = 8
HALF = QS * BS
PART = QB * MROWS
LIST0 = 4 * PART
SMALL = LIST0 + 16
F32 = jnp.float32
BF16 = jnp.bfloat16

SMEM = pl.BlockSpec(memory_space=pltpu.SMEM)
VMEM = pl.BlockSpec(memory_space=pltpu.VMEM)
PARAMS = pltpu.CompilerParams(vmem_limit_bytes=14 << 20)


def ring(n, k):
    return [(i, (i + k) % n) for i in range(n)]


def back(i, k):
    return lax.rem(i - k + 4, 4)


def pack_kernel(lists, counts, metric, out):
    out[0:PART, :] = metric[...]
    slot = lax.broadcasted_iota(jnp.int32, (NA, QS), 1)
    marked = jnp.where(slot < counts[...], lists[...], QB)
    tail = jnp.concatenate([marked, jnp.zeros((NA, AUXB - QS), jnp.int32)], axis=1)
    tail = jnp.concatenate([tail, jnp.zeros((8 - NA, AUXB), jnp.int32)], axis=0)
    out[PART : PART + 8, :] = tail.astype(F32).astype(BF16)


def pack(aux_list, aux_count, metric):
    return pl.pallas_call(
        pack_kernel,
        out_shape=jax.ShapeDtypeStruct((PART + 8, AUXB), BF16),
        in_specs=[VMEM] * 3,
        out_specs=VMEM,
        compiler_params=PARAMS,
        name="pack",
    )(aux_list, aux_count, metric)


def line_kernel(sc_ref, m0, m1, m2, m3, out):
    zh = sc_ref[1]
    parts = [m[...].astype(F32) for m in (m0, m1, m2, m3)]
    rows = lax.broadcasted_iota(jnp.int32, (8, AUXB), 0)
    tail = jnp.zeros((8, AUXB), F32)
    for src in range(4):
        k = back(zh, src)
        near = jnp.where(k == 0, parts[0], parts[1])
        far = jnp.where(k == 2, parts[2], parts[3])
        part = jnp.where(k < 2, near, far)
        for q in range(QB):
            at = (4 * q + src) * MROWS
            out[at : at + MROWS, :] = part[q * MROWS : (q + 1) * MROWS, :].astype(BF16)
        for a in range(NA):
            tail = jnp.where(rows == NA * src + a, part[PART + a : PART + a + 1, :], tail)
    both = jnp.concatenate([tail, parts[0][PART : PART + 8, :]], axis=0)
    out[LIST0:SMALL, :] = both.astype(BF16)


def line(sc, parts):
    return pl.pallas_call(
        line_kernel,
        out_shape=jax.ShapeDtypeStruct((SMALL, AUXB), BF16),
        in_specs=[SMEM] + [VMEM] * 4,
        out_specs=VMEM,
        compiler_params=PARAMS,
        name="line",
    )(sc, *parts)


def fill(tiles, start, met, lists, row, dense, base):
    for i in range(QS):
        q = lists[row, i]
        at = start + i * BS
        fitted = jnp.dot(tiles[at : at + BS, :], met[q], preferred_element_type=F32)
        cols = pl.ds(pl.multiple_of(q * AUXB, AUXB), AUXB)
        dense[pl.ds(pl.multiple_of(base, BS), BS), cols] = fitted.astype(BF16)


def fill_block(tiles, met, lists, row, dense, base):
    for a in range(NA):
        fill(tiles, a * HALF, met, lists, row + a, dense, base + a * BS)


def read_lists(small):
    return small[LIST0:SMALL, :].astype(F32).astype(jnp.int32)


def build_kernel(sc_ref, t0, t1, t2, t3, z1, z3, f1, f3, s0, s1, s2, s3, dy, dz, met, lv, ls, sem):
    y, zh = sc_ref[0], sc_ref[1]
    for k, s in enumerate((s0, s1, s2, s3)):
        lv[16 * k : 16 * k + 16, :] = read_lists(s)
    copy = pltpu.make_async_copy(lv, ls, sem)
    copy.start()
    for k, s in enumerate((s0, s1, s2, s3)):
        at = pl.multiple_of(back(y, k) * 4 * MROWS, 4 * MROWS)
        met[0:QB, pl.ds(at, 4 * MROWS), :] = s[0:LIST0, :].reshape(QB, 4 * MROWS, AUXB)
    dy[...] = jnp.zeros_like(dy)
    dz[...] = jnp.zeros_like(dz)
    copy.wait()
    fill_block(t0, met, ls, 8, dy, y * ROWS)
    mine = dy[pl.ds(pl.multiple_of(y * ROWS, ROWS), ROWS), :]
    dz[pl.ds(pl.multiple_of(zh * ROWS, ROWS), ROWS), :] = mine
    for k, t in ((1, t1), (2, t2), (3, t3)):
        fill_block(t, met, ls, 16 * k + 8, dy, back(y, k) * ROWS)
    for k, t in ((1, z1), (3, z3)):
        src = back(zh, k)
        fill_block(t, met, ls, NA * src, dz, src * ROWS)
    src = back(zh, 2)
    for a, f in enumerate((f1, f3)):
        fill(f, 0, met, ls, NA * src + a, dz, src * ROWS + a * BS)


def build(sc, tiles, zs, smalls):
    dense = jax.ShapeDtypeStruct((4 * ROWS, WIDE), BF16)
    return pl.pallas_call(
        build_kernel,
        out_shape=(dense, dense),
        in_specs=[SMEM] + [VMEM] * 12,
        out_specs=(VMEM,) * 2,
        scratch_shapes=[
            pltpu.VMEM((QB + 1, AUXB, AUXB), BF16),
            pltpu.VMEM((64, 128), jnp.int32),
            pltpu.SMEM((64, 128), jnp.int32),
            pltpu.SemaphoreType.DMA,
        ],
        compiler_params=PARAMS,
        name="build",
    )(sc, *tiles, *zs, *smalls)


def gram_kernel(flip, sc_ref, dy, dz, out):
    zh, co = sc_ref[1], sc_ref[2]
    parity = 1 - co if flip else co
    opposite = back(zh, 2)
    factor = 1.0 / (QS * 16 * AUXB) ** 0.5
    for h in range(2):
        p = 2 * h + parity
        block = dz[pl.ds(pl.multiple_of(p * ROWS, ROWS), ROWS), 0:USED]

        def product(swapped):
            for q in range(4):
                row = dy[q * ROWS : (q + 1) * ROWS, 0:USED]
                pair = (block, row) if swapped else (row, block)
                prod = lax.dot_general(*pair, (((1,), (1,)), ((), ())), preferred_element_type=F32)
                out[q, h] = prod * factor

        pl.when(p == opposite)(lambda: product(True))
        pl.when(p != opposite)(lambda: product(False))


def gram(flip, sc, dy, dz):
    return pl.pallas_call(
        functools.partial(gram_kernel, flip),
        out_shape=jax.ShapeDtypeStruct((4, 2, ROWS, ROWS), F32),
        in_specs=[SMEM] + [VMEM] * 2,
        out_specs=VMEM,
        compiler_params=PARAMS,
        name="send" if flip else "keep",
    )(sc, dy, dz)


def hold_kernel(tiles, late, out):
    out[...] = tiles[...]


def hold(tiles, late):
    return pl.pallas_call(
        hold_kernel,
        out_shape=jax.ShapeDtypeStruct(tiles.shape, tiles.dtype),
        in_specs=[VMEM] * 2,
        out_specs=VMEM,
        compiler_params=PARAMS,
        name="hold",
    )(tiles, late)


STEPS = tuple((k, w) for w in range(2) for k in range(4))


def share_kernel(sc_ref, keep, got, own, *outs):
    x, zl = sc_ref[3], sc_ref[4]
    for (k, w), out in zip(STEPS, (own,) + outs):
        q, h = lax.rem(x + k, 4), lax.rem(zl + w, 2)
        out[...] = (keep[q, h] + got[q, h]).astype(out.dtype)


def share(sc, keep, got):
    piece = (ROWS, ROWS)
    return pl.pallas_call(
        share_kernel,
        out_shape=(jax.ShapeDtypeStruct(piece, F32),) + (jax.ShapeDtypeStruct(piece, BF16),) * 7,
        in_specs=[SMEM, VMEM, VMEM],
        out_specs=(VMEM,) * 8,
        compiler_params=PARAMS,
        name="share",
    )(sc, keep, got)


def hop(k, w):
    return [(2 * a + b, 2 * ((a + k) % 4) + (b + w) % 2) for a in range(4) for b in range(2)]


def homes():
    moves = []
    for n in range(256):
        y, z, x, p = n // 64, n // 16 % 4, n // 4 % 4, n % 4
        home = (x, z, y, p) if p == (z + 2) % 4 else (y, p, x, z)
        moves.append((n, home[0] * 64 + home[1] * 16 + home[2] * 4 + home[3]))
    return moves


def local(fit_tiles, aux_list, aux_count, metric):
    sc = jnp.stack([lax.axis_index(n) for n in ("y", "zh", "co", "x", "zl")]).astype(jnp.int32)
    part = pack(aux_list, aux_count, metric.reshape(PART, AUXB))
    parts = [part] + [lax.ppermute(part, "zh", ring(4, k)) for k in (1, 2, 3)]
    tiles = fit_tiles.reshape(2 * HALF, AUXB)
    z1 = lax.ppermute(tiles, "zh", ring(4, 1))
    z3 = lax.ppermute(tiles, "zh", ring(4, 3))
    ys = [tiles] + [lax.ppermute(tiles, "y", ring(4, k)) for k in (1, 2, 3)]
    small = line(sc, parts)
    smalls = [small] + [lax.ppermute(small, "y", ring(4, k)) for k in (1, 2, 3)]
    f1 = lax.ppermute(z1[:HALF], "zh", ring(4, 1))
    f3 = lax.ppermute(z3[HALF:], "zh", ring(4, 3))

    mine = hold(tiles, part)
    dy, dz = build(sc, [mine] + ys[1:], [z1, z3, f1, f3], smalls)
    send = gram(True, sc, dy, dz)
    got = lax.ppermute(send, "co", ring(2, 1))
    keep = gram(False, sc, dy, dz)
    total, *shares = share(sc, keep, got)
    for (k, w), piece in zip(STEPS[1:], shares):
        total = total + lax.ppermute(piece, ("x", "zl"), hop(k, w)).astype(F32)
    return lax.ppermute(total, ("y", "zh", "x", "zl", "co"), homes())


def solution(mesh):
    fine = Mesh(mesh.devices.reshape(4, 4, 4, 2, 2), ("y", "zh", "x", "zl", "co"))
    row, col = ("y", "zh"), ("x", "zl", "co")
    placed = (P(row, col, None, None), P(row, col), P(row, col), P(col, row, None))

    return jax.shard_map(local, mesh=fine, in_specs=placed, out_specs=P(col, row), check_vma=False)
```

```python
import functools

import jax
import jax.numpy as jnp
from jax import lax
from jax.experimental import pallas as pl
from jax.experimental.pallas import tpu as pltpu
from jax.sharding import Mesh, PartitionSpec as P


AUXB = 128
BS = 128
QS = 6
QB = 12
NA = 2
ROWS = NA * BS
WIDE = (QB + 1) * AUXB
USED = QB * AUXB
MROWS = 8
HALF = QS * BS
PART = QB * MROWS
LIST0 = 4 * PART
SMALL = LIST0 + 16
F32 = jnp.float32
BF16 = jnp.bfloat16

SMEM = pl.BlockSpec(memory_space=pltpu.SMEM)
VMEM = pl.BlockSpec(memory_space=pltpu.VMEM)
PARAMS = pltpu.CompilerParams(vmem_limit_bytes=14 << 20)


def ring(n, k):
    return [(i, (i + k) % n) for i in range(n)]


def back(i, k):
    return lax.rem(i - k + 4, 4)


def pack_kernel(lists, counts, metric, out):
    out[0:PART, :] = metric[...]
    slot = lax.broadcasted_iota(jnp.int32, (NA, QS), 1)
    marked = jnp.where(slot < counts[...], lists[...], QB)
    tail = jnp.concatenate([marked, jnp.zeros((NA, AUXB - QS), jnp.int32)], axis=1)
    tail = jnp.concatenate([tail, jnp.zeros((8 - NA, AUXB), jnp.int32)], axis=0)
    out[PART : PART + 8, :] = tail.astype(F32).astype(BF16)


def pack(aux_list, aux_count, metric):
    return pl.pallas_call(
        pack_kernel,
        out_shape=jax.ShapeDtypeStruct((PART + 8, AUXB), BF16),
        in_specs=[VMEM] * 3,
        out_specs=VMEM,
        compiler_params=PARAMS,
        name="pack",
    )(aux_list, aux_count, metric)


def line_kernel(sc_ref, m0, m1, m2, m3, out):
    zh = sc_ref[1]
    parts = [m[...].astype(F32) for m in (m0, m1, m2, m3)]
    rows = lax.broadcasted_iota(jnp.int32, (8, AUXB), 0)
    tail = jnp.zeros((8, AUXB), F32)
    for src in range(4):
        k = back(zh, src)
        near = jnp.where(k == 0, parts[0], parts[1])
        far = jnp.where(k == 2, parts[2], parts[3])
        part = jnp.where(k < 2, near, far)
        for q in range(QB):
            at = (4 * q + src) * MROWS
            out[at : at + MROWS, :] = part[q * MROWS : (q + 1) * MROWS, :].astype(BF16)
        for a in range(NA):
            tail = jnp.where(rows == NA * src + a, part[PART + a : PART + a + 1, :], tail)
    both = jnp.concatenate([tail, parts[0][PART : PART + 8, :]], axis=0)
    out[LIST0:SMALL, :] = both.astype(BF16)


def line(sc, parts):
    return pl.pallas_call(
        line_kernel,
        out_shape=jax.ShapeDtypeStruct((SMALL, AUXB), BF16),
        in_specs=[SMEM] + [VMEM] * 4,
        out_specs=VMEM,
        compiler_params=PARAMS,
        name="line",
    )(sc, *parts)


def fill(tiles, start, met, lists, row, dense, base):
    for i in range(QS):
        q = lists[row, i]
        at = start + i * BS
        fitted = jnp.dot(tiles[at : at + BS, :], met[q], preferred_element_type=F32)
        cols = pl.ds(pl.multiple_of(q * AUXB, AUXB), AUXB)
        dense[pl.ds(pl.multiple_of(base, BS), BS), cols] = fitted.astype(BF16)


def fill_block(tiles, met, lists, row, dense, base):
    for a in range(NA):
        fill(tiles, a * HALF, met, lists, row + a, dense, base + a * BS)


def read_lists(small):
    return small[LIST0:SMALL, :].astype(F32).astype(jnp.int32)


def build_kernel(sc_ref, t0, t1, t2, t3, z1, z3, f1, f3, s0, s1, s2, s3, ey, ez, dy, dz, met, lv, ls, sem):
    y, zh = sc_ref[0], sc_ref[1]
    for k, s in enumerate((s0, s1, s2, s3)):
        lv[16 * k : 16 * k + 16, :] = read_lists(s)
    copy = pltpu.make_async_copy(lv, ls, sem)
    copy.start()
    for k, s in enumerate((s0, s1, s2, s3)):
        at = pl.multiple_of(back(y, k) * 4 * MROWS, 4 * MROWS)
        met[0:QB, pl.ds(at, 4 * MROWS), :] = s[0:LIST0, :].reshape(QB, 4 * MROWS, AUXB)
    copy.wait()
    fill_block(t0, met, ls, 8, dy, y * ROWS)
    mine = dy[pl.ds(pl.multiple_of(y * ROWS, ROWS), ROWS), :]
    dz[pl.ds(pl.multiple_of(zh * ROWS, ROWS), ROWS), :] = mine
    for k, t in ((1, t1), (2, t2), (3, t3)):
        fill_block(t, met, ls, 16 * k + 8, dy, back(y, k) * ROWS)
    for k, t in ((1, z1), (3, z3)):
        src = back(zh, k)
        fill_block(t, met, ls, NA * src, dz, src * ROWS)
    src = back(zh, 2)
    for a, f in enumerate((f1, f3)):
        fill(f, 0, met, ls, NA * src + a, dz, src * ROWS + a * BS)


def build(sc, tiles, zs, smalls, empty):
    dense = jax.ShapeDtypeStruct((4 * ROWS, WIDE), BF16)
    return pl.pallas_call(
        build_kernel,
        out_shape=(dense, dense),
        in_specs=[SMEM] + [VMEM] * 14,
        out_specs=(VMEM,) * 2,
        scratch_shapes=[
            pltpu.VMEM((QB + 1, AUXB, AUXB), BF16),
            pltpu.VMEM((64, 128), jnp.int32),
            pltpu.SMEM((64, 128), jnp.int32),
            pltpu.SemaphoreType.DMA,
        ],
        input_output_aliases={13: 0, 14: 1},
        compiler_params=PARAMS,
        name="build",
    )(sc, *tiles, *zs, *smalls, *empty)


def gram_kernel(flip, sc_ref, dy, dz, out):
    zh, co = sc_ref[1], sc_ref[2]
    parity = 1 - co if flip else co
    opposite = back(zh, 2)
    factor = 1.0 / (QS * 16 * AUXB) ** 0.5
    for h in range(2):
        p = 2 * h + parity
        block = dz[pl.ds(pl.multiple_of(p * ROWS, ROWS), ROWS), 0:USED]

        @pl.when(p == opposite)
        def _():
            for q in range(4):
                row = dy[q * ROWS : (q + 1) * ROWS, 0:USED]
                prod = lax.dot_general(
                    block, row, (((1,), (1,)), ((), ())), preferred_element_type=F32
                )
                out[q, h] = prod * factor

        @pl.when(p != opposite)
        def _():
            prod = lax.dot_general(
                dy[:, 0:USED], block, (((1,), (1,)), ((), ())), preferred_element_type=F32
            )
            for q in range(4):
                out[q, h] = prod[q * ROWS : (q + 1) * ROWS, :] * factor


def gram(flip, sc, dy, dz):
    return pl.pallas_call(
        functools.partial(gram_kernel, flip),
        out_shape=jax.ShapeDtypeStruct((4, 2, ROWS, ROWS), F32),
        in_specs=[SMEM] + [VMEM] * 2,
        out_specs=VMEM,
        compiler_params=PARAMS,
        name="send" if flip else "keep",
    )(sc, dy, dz)


def hold_kernel(tiles, late, out, dy, dz):
    out[...] = tiles[...]
    dy[...] = jnp.zeros_like(dy)
    dz[...] = jnp.zeros_like(dz)


def hold(tiles, late):
    dense = jax.ShapeDtypeStruct((4 * ROWS, WIDE), BF16)
    return pl.pallas_call(
        hold_kernel,
        out_shape=(jax.ShapeDtypeStruct(tiles.shape, tiles.dtype), dense, dense),
        in_specs=[VMEM] * 2,
        out_specs=(VMEM,) * 3,
        compiler_params=PARAMS,
        name="hold",
    )(tiles, late)


STEPS = tuple((k, w) for w in range(2) for k in range(4))


def share_kernel(sc_ref, keep, got, own, *outs):
    x, zl = sc_ref[3], sc_ref[4]
    for (k, w), out in zip(STEPS, (own,) + outs):
        q, h = lax.rem(x + k, 4), lax.rem(zl + w, 2)
        out[...] = (keep[q, h] + got[q, h]).astype(out.dtype)


def share(sc, keep, got):
    piece = (ROWS, ROWS)
    return pl.pallas_call(
        share_kernel,
        out_shape=(jax.ShapeDtypeStruct(piece, F32),) + (jax.ShapeDtypeStruct(piece, BF16),) * 7,
        in_specs=[SMEM, VMEM, VMEM],
        out_specs=(VMEM,) * 8,
        compiler_params=PARAMS,
        name="share",
    )(sc, keep, got)


def hop(k, w):
    return [(2 * a + b, 2 * ((a + k) % 4) + (b + w) % 2) for a in range(4) for b in range(2)]


def homes():
    moves = []
    for n in range(256):
        y, z, x, p = n // 64, n // 16 % 4, n // 4 % 4, n % 4
        home = (x, z, y, p) if p == (z + 2) % 4 else (y, p, x, z)
        moves.append((n, home[0] * 64 + home[1] * 16 + home[2] * 4 + home[3]))
    return moves


def local(fit_tiles, aux_list, aux_count, metric):
    sc = jnp.stack([lax.axis_index(n) for n in ("y", "zh", "co", "x", "zl")]).astype(jnp.int32)
    part = pack(aux_list, aux_count, metric.reshape(PART, AUXB))
    parts = [part] + [lax.ppermute(part, "zh", ring(4, k)) for k in (1, 2, 3)]
    tiles = fit_tiles.reshape(2 * HALF, AUXB)
    z1 = lax.ppermute(tiles, "zh", ring(4, 1))
    z3 = lax.ppermute(tiles, "zh", ring(4, 3))
    ys = [tiles] + [lax.ppermute(tiles, "y", ring(4, k)) for k in (1, 2, 3)]
    small = line(sc, parts)
    smalls = [small] + [lax.ppermute(small, "y", ring(4, k)) for k in (1, 2, 3)]
    f1 = lax.ppermute(z1[:HALF], "zh", ring(4, 1))
    f3 = lax.ppermute(z3[HALF:], "zh", ring(4, 3))

    mine, *empty = hold(tiles, part)
    dy, dz = build(sc, [mine] + ys[1:], [z1, z3, f1, f3], smalls, empty)
    send = gram(True, sc, dy, dz)
    got = lax.ppermute(send, "co", ring(2, 1))
    keep = gram(False, sc, dy, dz)
    total, *shares = share(sc, keep, got)
    for (k, w), piece in zip(STEPS[1:], shares):
        total = total + lax.ppermute(piece, ("x", "zl"), hop(k, w)).astype(F32)
    return lax.ppermute(total, ("y", "zh", "x", "zl", "co"), homes())


def solution(mesh):
    fine = Mesh(mesh.devices.reshape(4, 4, 4, 2, 2), ("y", "zh", "x", "zl", "co"))
    row, col = ("y", "zh"), ("x", "zl", "co")
    placed = (P(row, col, None, None), P(row, col), P(row, col), P(col, row, None))

    return jax.shard_map(local, mesh=fine, in_specs=placed, out_specs=P(col, row), check_vma=False)
```

```python
import functools

import jax
import jax.numpy as jnp
from jax import lax
from jax.experimental import pallas as pl
from jax.experimental.pallas import tpu as pltpu
from jax.sharding import Mesh, PartitionSpec as P


AUXB = 128
BS = 128
QS = 6
QB = 12
NA = 2
ROWS = NA * BS
WIDE = (QB + 1) * AUXB
USED = QB * AUXB
MROWS = 8
HALF = QS * BS
PART = QB * MROWS
LIST0 = 4 * PART
SMALL = LIST0 + 16
F32 = jnp.float32
BF16 = jnp.bfloat16

SMEM = pl.BlockSpec(memory_space=pltpu.SMEM)
VMEM = pl.BlockSpec(memory_space=pltpu.VMEM)
PARAMS = pltpu.CompilerParams(vmem_limit_bytes=14 << 20)


def ring(n, k):
    return [(i, (i + k) % n) for i in range(n)]


def back(i, k):
    return lax.rem(i - k + 4, 4)


def pack_kernel(lists, counts, metric, out):
    out[0:PART, :] = metric[...]
    slot = lax.broadcasted_iota(jnp.int32, (NA, QS), 1)
    marked = jnp.where(slot < counts[...], lists[...], QB)
    tail = jnp.concatenate([marked, jnp.zeros((NA, AUXB - QS), jnp.int32)], axis=1)
    tail = jnp.concatenate([tail, jnp.zeros((8 - NA, AUXB), jnp.int32)], axis=0)
    out[PART : PART + 8, :] = tail.astype(F32).astype(BF16)


def pack(aux_list, aux_count, metric):
    return pl.pallas_call(
        pack_kernel,
        out_shape=jax.ShapeDtypeStruct((PART + 8, AUXB), BF16),
        in_specs=[VMEM] * 3,
        out_specs=VMEM,
        compiler_params=PARAMS,
        name="pack",
    )(aux_list, aux_count, metric)


def line_kernel(sc_ref, m0, m1, m2, m3, out):
    zh = sc_ref[1]
    parts = [m[...].astype(F32) for m in (m0, m1, m2, m3)]
    rows = lax.broadcasted_iota(jnp.int32, (8, AUXB), 0)
    tail = jnp.zeros((8, AUXB), F32)
    for src in range(4):
        k = back(zh, src)
        near = jnp.where(k == 0, parts[0], parts[1])
        far = jnp.where(k == 2, parts[2], parts[3])
        part = jnp.where(k < 2, near, far)
        for q in range(QB):
            at = (4 * q + src) * MROWS
            out[at : at + MROWS, :] = part[q * MROWS : (q + 1) * MROWS, :].astype(BF16)
        for a in range(NA):
            tail = jnp.where(rows == NA * src + a, part[PART + a : PART + a + 1, :], tail)
    both = jnp.concatenate([tail, parts[0][PART : PART + 8, :]], axis=0)
    out[LIST0:SMALL, :] = both.astype(BF16)


def line(sc, parts):
    return pl.pallas_call(
        line_kernel,
        out_shape=jax.ShapeDtypeStruct((SMALL, AUXB), BF16),
        in_specs=[SMEM] + [VMEM] * 4,
        out_specs=VMEM,
        compiler_params=PARAMS,
        name="line",
    )(sc, *parts)


def fill(tiles, start, met, lists, row, dense, base):
    for i in range(QS):
        q = lists[row, i]
        at = start + i * BS
        fitted = jnp.dot(tiles[at : at + BS, :], met[q], preferred_element_type=F32)
        cols = pl.ds(pl.multiple_of(q * AUXB, AUXB), AUXB)
        dense[pl.ds(pl.multiple_of(base, BS), BS), cols] = fitted.astype(BF16)


def fill_block(tiles, met, lists, row, dense, base):
    for a in range(NA):
        fill(tiles, a * HALF, met, lists, row + a, dense, base + a * BS)


def read_lists(small):
    return small[LIST0:SMALL, :].astype(F32).astype(jnp.int32)


def build_kernel(sc_ref, t0, t1, t2, t3, z1, z3, f1, f3, s0, s1, s2, s3, dy, dz, met, lv, ls, sem):
    y, zh = sc_ref[0], sc_ref[1]
    for k, s in enumerate((s0, s1, s2, s3)):
        lv[16 * k : 16 * k + 16, :] = read_lists(s)
    copy = pltpu.make_async_copy(lv, ls, sem)
    copy.start()
    for k, s in enumerate((s0, s1, s2, s3)):
        at = pl.multiple_of(back(y, k) * 4 * MROWS, 4 * MROWS)
        met[0:QB, pl.ds(at, 4 * MROWS), :] = s[0:LIST0, :].reshape(QB, 4 * MROWS, AUXB)
    dy[...] = jnp.zeros_like(dy)
    dz[...] = jnp.zeros_like(dz)
    copy.wait()
    fill_block(t0, met, ls, 8, dy, y * ROWS)
    mine = dy[pl.ds(pl.multiple_of(y * ROWS, ROWS), ROWS), :]
    dz[pl.ds(pl.multiple_of(zh * ROWS, ROWS), ROWS), :] = mine
    for k, t in ((1, t1), (2, t2), (3, t3)):
        fill_block(t, met, ls, 16 * k + 8, dy, back(y, k) * ROWS)
    for k, t in ((1, z1), (3, z3)):
        src = back(zh, k)
        fill_block(t, met, ls, NA * src, dz, src * ROWS)
    src = back(zh, 2)
    for a, f in enumerate((f1, f3)):
        fill(f, 0, met, ls, NA * src + a, dz, src * ROWS + a * BS)


def build(sc, tiles, zs, smalls):
    dense = jax.ShapeDtypeStruct((4 * ROWS, WIDE), BF16)
    return pl.pallas_call(
        build_kernel,
        out_shape=(dense, dense),
        in_specs=[SMEM] + [VMEM] * 12,
        out_specs=(VMEM,) * 2,
        scratch_shapes=[
            pltpu.VMEM((QB + 1, AUXB, AUXB), BF16),
            pltpu.VMEM((64, 128), jnp.int32),
            pltpu.SMEM((64, 128), jnp.int32),
            pltpu.SemaphoreType.DMA,
        ],
        compiler_params=PARAMS,
        name="build",
    )(sc, *tiles, *zs, *smalls)


def gram_kernel(flip, picks, sc_ref, dy, dz, out):
    zh, co = sc_ref[1], sc_ref[2]
    parity = 1 - co if flip else co
    opposite = back(zh, 2)
    factor = 1.0 / (QS * 16 * AUXB) ** 0.5
    for slot, h in enumerate(picks):
        p = 2 * h + parity
        block = dz[pl.ds(pl.multiple_of(p * ROWS, ROWS), ROWS), 0:USED]

        def product(swapped, block=block, slot=slot):
            for q in range(4):
                row = dy[q * ROWS : (q + 1) * ROWS, 0:USED]
                pair = (block, row) if swapped else (row, block)
                prod = lax.dot_general(*pair, (((1,), (1,)), ((), ())), preferred_element_type=F32)
                out[q, slot] = prod * factor

        pl.when(p == opposite)(lambda: product(True))
        pl.when(p != opposite)(lambda: product(False))


def gram(flip, picks, sc, dy, dz):
    return pl.pallas_call(
        functools.partial(gram_kernel, flip, picks),
        out_shape=jax.ShapeDtypeStruct((4, len(picks), ROWS, ROWS), F32),
        in_specs=[SMEM] + [VMEM] * 2,
        out_specs=VMEM,
        compiler_params=PARAMS,
    )(sc, dy, dz)


def hold_kernel(tiles, late, out):
    out[...] = tiles[...]


def hold(tiles, late):
    return pl.pallas_call(
        hold_kernel,
        out_shape=jax.ShapeDtypeStruct(tiles.shape, tiles.dtype),
        in_specs=[VMEM] * 2,
        out_specs=VMEM,
        compiler_params=PARAMS,
        name="hold",
    )(tiles, late)


STEPS = tuple((k, w) for w in range(2) for k in range(4))


def share_kernel(sc_ref, keep, got0, got1, *outs):
    x, zl = sc_ref[3], sc_ref[4]

    def write(low):
        for (k, w), out in zip(STEPS, outs):
            q, h = lax.rem(x + k, 4), w if low else 1 - w
            got = got1 if h else got0
            out[...] = (keep[q, h] + got[q, 0]).astype(out.dtype)

    pl.when(zl == 0)(lambda: write(True))
    pl.when(zl != 0)(lambda: write(False))


def share(sc, keep, got0, got1):
    piece = (ROWS, ROWS)
    return pl.pallas_call(
        share_kernel,
        out_shape=(jax.ShapeDtypeStruct(piece, F32),) + (jax.ShapeDtypeStruct(piece, BF16),) * 7,
        in_specs=[SMEM] + [VMEM] * 3,
        out_specs=(VMEM,) * 8,
        compiler_params=PARAMS,
        name="share",
    )(sc, keep, got0, got1)


def hop(k, w):
    return [(2 * a + b, 2 * ((a + k) % 4) + (b + w) % 2) for a in range(4) for b in range(2)]


def homes():
    moves = []
    for n in range(256):
        y, z, x, p = n // 64, n // 16 % 4, n // 4 % 4, n % 4
        home = (x, z, y, p) if p == (z + 2) % 4 else (y, p, x, z)
        moves.append((n, home[0] * 64 + home[1] * 16 + home[2] * 4 + home[3]))
    return moves


def local(fit_tiles, aux_list, aux_count, metric):
    sc = jnp.stack([lax.axis_index(n) for n in ("y", "zh", "co", "x", "zl")]).astype(jnp.int32)
    part = pack(aux_list, aux_count, metric.reshape(PART, AUXB))
    parts = [part] + [lax.ppermute(part, "zh", ring(4, k)) for k in (1, 2, 3)]
    tiles = fit_tiles.reshape(2 * HALF, AUXB)
    z1 = lax.ppermute(tiles, "zh", ring(4, 1))
    z3 = lax.ppermute(tiles, "zh", ring(4, 3))
    ys = [tiles] + [lax.ppermute(tiles, "y", ring(4, k)) for k in (1, 2, 3)]
    small = line(sc, parts)
    smalls = [small] + [lax.ppermute(small, "y", ring(4, k)) for k in (1, 2, 3)]
    f1 = lax.ppermute(z1[:HALF], "zh", ring(4, 1))
    f3 = lax.ppermute(z3[HALF:], "zh", ring(4, 3))

    mine = hold(tiles, part)
    dy, dz = build(sc, [mine] + ys[1:], [z1, z3, f1, f3], smalls)
    got = []
    for h in range(2):
        send = gram(True, (h,), sc, dy, dz)
        got.append(lax.ppermute(send, "co", ring(2, 1)))
    keep = gram(False, (0, 1), sc, dy, dz)
    total, *shares = share(sc, keep, *got)
    for (k, w), piece in zip(STEPS[1:], shares):
        total = total + lax.ppermute(piece, ("x", "zl"), hop(k, w)).astype(F32)
    return lax.ppermute(total, ("y", "zh", "x", "zl", "co"), homes())


def solution(mesh):
    fine = Mesh(mesh.devices.reshape(4, 4, 4, 2, 2), ("y", "zh", "x", "zl", "co"))
    row, col = ("y", "zh"), ("x", "zl", "co")
    placed = (P(row, col, None, None), P(row, col), P(row, col), P(col, row, None))

    return jax.shard_map(local, mesh=fine, in_specs=placed, out_specs=P(col, row), check_vma=False)
```

```python
import functools

import jax
import jax.numpy as jnp
from jax import lax
from jax.experimental import pallas as pl
from jax.experimental.pallas import tpu as pltpu
from jax.sharding import Mesh, PartitionSpec as P


AUXB = 128
BS = 128
QS = 6
QB = 12
NA = 2
ROWS = NA * BS
WIDE = (QB + 1) * AUXB
USED = QB * AUXB
MROWS = 8
HALF = QS * BS
PART = QB * MROWS
LIST0 = 4 * PART
SMALL = LIST0 + 16
F32 = jnp.float32
BF16 = jnp.bfloat16

SMEM = pl.BlockSpec(memory_space=pltpu.SMEM)
VMEM = pl.BlockSpec(memory_space=pltpu.VMEM)
PARAMS = pltpu.CompilerParams(vmem_limit_bytes=14 << 20)


def ring(n, k):
    return [(i, (i + k) % n) for i in range(n)]


def back(i, k):
    return lax.rem(i - k + 4, 4)


def pack_kernel(lists, counts, metric, out):
    out[0:PART, :] = metric[...]
    slot = lax.broadcasted_iota(jnp.int32, (NA, QS), 1)
    marked = jnp.where(slot < counts[...], lists[...], QB)
    tail = jnp.concatenate([marked, jnp.zeros((NA, AUXB - QS), jnp.int32)], axis=1)
    tail = jnp.concatenate([tail, jnp.zeros((8 - NA, AUXB), jnp.int32)], axis=0)
    out[PART : PART + 8, :] = tail.astype(F32).astype(BF16)


def pack(aux_list, aux_count, metric):
    return pl.pallas_call(
        pack_kernel,
        out_shape=jax.ShapeDtypeStruct((PART + 8, AUXB), BF16),
        in_specs=[VMEM] * 3,
        out_specs=VMEM,
        compiler_params=PARAMS,
        name="pack",
    )(aux_list, aux_count, metric)


def line_kernel(sc_ref, m0, m1, m2, m3, out):
    zh = sc_ref[1]
    parts = [m[...].astype(F32) for m in (m0, m1, m2, m3)]
    rows = lax.broadcasted_iota(jnp.int32, (8, AUXB), 0)
    tail = jnp.zeros((8, AUXB), F32)
    for src in range(4):
        k = back(zh, src)
        near = jnp.where(k == 0, parts[0], parts[1])
        far = jnp.where(k == 2, parts[2], parts[3])
        part = jnp.where(k < 2, near, far)
        for q in range(QB):
            at = (4 * q + src) * MROWS
            out[at : at + MROWS, :] = part[q * MROWS : (q + 1) * MROWS, :].astype(BF16)
        for a in range(NA):
            tail = jnp.where(rows == NA * src + a, part[PART + a : PART + a + 1, :], tail)
    both = jnp.concatenate([tail, parts[0][PART : PART + 8, :]], axis=0)
    out[LIST0:SMALL, :] = both.astype(BF16)


def line(sc, parts):
    return pl.pallas_call(
        line_kernel,
        out_shape=jax.ShapeDtypeStruct((SMALL, AUXB), BF16),
        in_specs=[SMEM] + [VMEM] * 4,
        out_specs=VMEM,
        compiler_params=PARAMS,
        name="line",
    )(sc, *parts)


def fill(tiles, start, met, lists, row, dense, base):
    for i in range(QS):
        q = lists[row, i]
        at = start + i * BS
        fitted = jnp.dot(tiles[at : at + BS, :], met[q], preferred_element_type=F32)
        cols = pl.ds(pl.multiple_of(q * AUXB, AUXB), AUXB)
        dense[pl.ds(pl.multiple_of(base, BS), BS), cols] = fitted.astype(BF16)


def fill_block(tiles, met, lists, row, dense, base):
    for a in range(NA):
        fill(tiles, a * HALF, met, lists, row + a, dense, base + a * BS)


def read_lists(small):
    return small[LIST0:SMALL, :].astype(F32).astype(jnp.int32)


def build_kernel(sc_ref, t0, t1, t2, t3, z1, z3, f1, f3, s0, s1, s2, s3, dy, dz, met, lv, ls, sem):
    y, zh = sc_ref[0], sc_ref[1]
    for k, s in enumerate((s0, s1, s2, s3)):
        lv[16 * k : 16 * k + 16, :] = read_lists(s)
    copy = pltpu.make_async_copy(lv, ls, sem)
    copy.start()
    for k, s in enumerate((s0, s1, s2, s3)):
        at = pl.multiple_of(back(y, k) * 4 * MROWS, 4 * MROWS)
        met[0:QB, pl.ds(at, 4 * MROWS), :] = s[0:LIST0, :].reshape(QB, 4 * MROWS, AUXB)
    dy[...] = jnp.zeros_like(dy)
    dz[...] = jnp.zeros_like(dz)
    copy.wait()
    fill_block(t0, met, ls, 8, dy, y * ROWS)
    mine = dy[pl.ds(pl.multiple_of(y * ROWS, ROWS), ROWS), :]
    dz[pl.ds(pl.multiple_of(zh * ROWS, ROWS), ROWS), :] = mine
    for k, t in ((1, t1), (2, t2), (3, t3)):
        fill_block(t, met, ls, 16 * k + 8, dy, back(y, k) * ROWS)
    for k, t in ((1, z1), (3, z3)):
        src = back(zh, k)
        fill_block(t, met, ls, NA * src, dz, src * ROWS)
    src = back(zh, 2)
    for a, f in enumerate((f1, f3)):
        fill(f, 0, met, ls, NA * src + a, dz, src * ROWS + a * BS)


def build(sc, tiles, zs, smalls):
    dense = jax.ShapeDtypeStruct((4 * ROWS, WIDE), BF16)
    return pl.pallas_call(
        build_kernel,
        out_shape=(dense, dense),
        in_specs=[SMEM] + [VMEM] * 12,
        out_specs=(VMEM,) * 2,
        scratch_shapes=[
            pltpu.VMEM((QB + 1, AUXB, AUXB), BF16),
            pltpu.VMEM((64, 128), jnp.int32),
            pltpu.SMEM((64, 128), jnp.int32),
            pltpu.SemaphoreType.DMA,
        ],
        compiler_params=PARAMS,
        name="build",
    )(sc, *tiles, *zs, *smalls)


def gram_kernel(flip, picks, sc_ref, dy, dz, out):
    zh, co = sc_ref[1], sc_ref[2]
    parity = 1 - co if flip else co
    opposite = back(zh, 2)
    factor = 1.0 / (QS * 16 * AUXB) ** 0.5
    for slot, h in enumerate(picks):
        p = 2 * h + parity
        block = dz[pl.ds(pl.multiple_of(p * ROWS, ROWS), ROWS), 0:USED]

        def product(swapped, block=block, slot=slot):
            for q in range(4):
                row = dy[q * ROWS : (q + 1) * ROWS, 0:USED]
                pair = (block, row) if swapped else (row, block)
                prod = lax.dot_general(*pair, (((1,), (1,)), ((), ())), preferred_element_type=F32)
                out[q, slot] = prod * factor

        pl.when(p == opposite)(lambda: product(True))
        pl.when(p != opposite)(lambda: product(False))


def gram(flip, picks, sc, dy, dz):
    return pl.pallas_call(
        functools.partial(gram_kernel, flip, picks),
        out_shape=jax.ShapeDtypeStruct((4, len(picks), ROWS, ROWS), F32),
        in_specs=[SMEM] + [VMEM] * 2,
        out_specs=VMEM,
        compiler_params=PARAMS,
    )(sc, dy, dz)


def hold_kernel(tiles, late, out):
    out[...] = tiles[...]


def hold(tiles, late):
    return pl.pallas_call(
        hold_kernel,
        out_shape=jax.ShapeDtypeStruct(tiles.shape, tiles.dtype),
        in_specs=[VMEM] * 2,
        out_specs=VMEM,
        compiler_params=PARAMS,
        name="hold",
    )(tiles, late)


FIRST = ((2, 1), (2, 0))
REST = ((1, 1), (3, 1), (1, 0), (3, 0), (0, 1), (0, 0))


def share_kernel(steps, sc_ref, keep, got0, got1, *outs):
    x, zl = sc_ref[3], sc_ref[4]

    def write(low):
        for (k, w), out in zip(steps, outs):
            q, h = lax.rem(x + k, 4), w if low else 1 - w
            got = got1 if h else got0
            out[...] = (keep[q, h] + got[q, 0]).astype(out.dtype)

    pl.when(zl == 0)(lambda: write(True))
    pl.when(zl != 0)(lambda: write(False))


def share(steps, sc, keep, got0, got1):
    kinds = [F32 if step == (0, 0) else BF16 for step in steps]
    return pl.pallas_call(
        functools.partial(share_kernel, steps),
        out_shape=tuple(jax.ShapeDtypeStruct((ROWS, ROWS), kind) for kind in kinds),
        in_specs=[SMEM] + [VMEM] * 3,
        out_specs=(VMEM,) * len(steps),
        compiler_params=PARAMS,
        name="share",
    )(sc, keep, got0, got1)


def hop(k, w):
    return [(2 * a + b, 2 * ((a + k) % 4) + (b + w) % 2) for a in range(4) for b in range(2)]


def homes():
    moves = []
    for n in range(256):
        y, z, x, p = n // 64, n // 16 % 4, n // 4 % 4, n % 4
        home = (x, z, y, p) if p == (z + 2) % 4 else (y, p, x, z)
        moves.append((n, home[0] * 64 + home[1] * 16 + home[2] * 4 + home[3]))
    return moves


def local(fit_tiles, aux_list, aux_count, metric):
    sc = jnp.stack([lax.axis_index(n) for n in ("y", "zh", "co", "x", "zl")]).astype(jnp.int32)
    part = pack(aux_list, aux_count, metric.reshape(PART, AUXB))
    parts = [part] + [lax.ppermute(part, "zh", ring(4, k)) for k in (1, 2, 3)]
    tiles = fit_tiles.reshape(2 * HALF, AUXB)
    z1 = lax.ppermute(tiles, "zh", ring(4, 1))
    z3 = lax.ppermute(tiles, "zh", ring(4, 3))
    ys = [tiles] + [lax.ppermute(tiles, "y", ring(4, k)) for k in (1, 2, 3)]
    small = line(sc, parts)
    smalls = [small] + [lax.ppermute(small, "y", ring(4, k)) for k in (1, 2, 3)]
    f1 = lax.ppermute(z1[:HALF], "zh", ring(4, 1))
    f3 = lax.ppermute(z3[HALF:], "zh", ring(4, 3))

    mine = hold(tiles, part)
    dy, dz = build(sc, [mine] + ys[1:], [z1, z3, f1, f3], smalls)
    got = []
    for h in range(2):
        send = gram(True, (h,), sc, dy, dz)
        got.append(lax.ppermute(send, "co", ring(2, 1)))
    keep = gram(False, (0, 1), sc, dy, dz)
    pieces = list(share(FIRST, sc, keep, *got))
    pieces += share(REST, sc, keep, *got)
    total = pieces.pop()
    for (k, w), piece in zip(FIRST + REST, pieces):
        total = total + lax.ppermute(piece, ("x", "zl"), hop(k, w)).astype(F32)
    return lax.ppermute(total, ("y", "zh", "x", "zl", "co"), homes())


def solution(mesh):
    fine = Mesh(mesh.devices.reshape(4, 4, 4, 2, 2), ("y", "zh", "x", "zl", "co"))
    row, col = ("y", "zh"), ("x", "zl", "co")
    placed = (P(row, col, None, None), P(row, col), P(row, col), P(col, row, None))

    return jax.shard_map(local, mesh=fine, in_specs=placed, out_specs=P(col, row), check_vma=False)
```
